128 devices in a mesh: grp: 2 (over x_hi), layer: 4 (over z), feat: 16 (over x_lo, y, core).
Axes of the slice: x: 4 (x_hi: 2, x_lo: 2; x = x_hi * 2 + x_lo), y: 4, z: 4, core: 2. Of those that a mesh axis runs over, the one named last changes fastest.
Arguments:
- inputs: bfloat16 [4, 2048, 2304], P('layer', ('grp', 'feat')), may hold values from -6 to 6
- targets: bfloat16 [2048, 4, 2304], P(('grp', 'feat'), None, 'layer'), may hold values from -6 to 6
- enc_weight: bfloat16 [4, 2304, 8192], P('layer', None, 'feat'), may hold values from -0.125 to 0.125
- enc_bias: float32 [4, 8192], P('layer', 'feat'), may hold values from -3 to 3
- dec_weight: bfloat16 [10, 8192, 2304], P(None, 'feat', 'layer'), may hold values from -0.0625 to 0.0625
- dec_bias: float32 [4, 2304], P(None, 'layer'), may hold values from -3 to 3
Outputs:
- enc_grad: bfloat16 [4, 2304, 8192], P('layer', 'grp', 'feat')
- enc_bias_grad: float32 [4, 8192], P('layer', 'feat')
- dec_grad: bfloat16 [10, 8192, 2304], P('grp', 'feat', 'layer')
- dec_bias_grad: float32 [4, 2304], P(None, 'layer')
The draws below stay inside these ranges and needn't reach their ends.
All inputs are finite; a program needn't handle non-finite values.
Results may differ from the reference program's by a relative error of at most 0.019.
Values may be sent and summed in bfloat16 or wider, within the bound.
No kernel may reach another device: no remote copies, remote signals or barrier semaphores. Data moves between devices by JAX's collectives and lax.ppermute only.
A program may use at most 128 MiB of HBM per device.

```python
import jax
import jax.numpy as jnp

D = 2304
FEATS = 8192
LAYERS = 4
PAIRS = 10
TOKENS = 2048


def block_scale(own_key, shape, pieces, least, top_value):
    level = 1.0
    for axis_at, parts in pieces:
        steps = jax.random.uniform(jax.random.fold_in(jax.random.fold_in(own_key, 6), axis_at), (parts,), jnp.float32, least / len(pieces), top_value / len(pieces))
        level = level * jnp.repeat(jnp.exp(steps), shape[axis_at] // parts).reshape((-1,) + (1,) * (len(shape) - 1 - axis_at))
    return level


def gaussian(rng, dims, deviation, bound, cuts=(), held_as=jnp.bfloat16):
    values = jax.random.normal(rng, dims, jnp.float32) * deviation
    if len(cuts) > 0:
        values = block_scale(rng, dims, cuts, -0.22, 0.18) * values
    return jnp.clip(values, min=-bound, max=bound).astype(held_as)


def setup_inputs(seed: int = 0) -> dict:
    streams_of = jax.random.split(jax.random.key(seed), 7)
    inputs = gaussian(streams_of[0], (LAYERS, TOKENS, D), 1.0, 6.0, ((0, 4), (1, 32)))
    targets = gaussian(streams_of[1], (TOKENS, LAYERS, D), 1.0, 6.0, ((0, 32), (2, 4)))
    enc_weight = gaussian(streams_of[2], (LAYERS, D, FEATS), D ** -0.5, 0.125, ((0, 4), (2, 16)))
    enc_bias = gaussian(streams_of[3], (LAYERS, FEATS), 0.5, 3.0, ((0, 4), (1, 16)), jnp.float32)
    dec_weight = gaussian(streams_of[4], (PAIRS, FEATS, D), FEATS ** -0.5, 0.0625, ((1, 16), (2, 4)))
    dec_bias = gaussian(streams_of[5], (LAYERS, D), 0.5, 3.0, ((1, 4),), jnp.float32)
    return dict(inputs=inputs, targets=targets, enc_weight=enc_weight, enc_bias=enc_bias, dec_weight=dec_weight, dec_bias=dec_bias)


def pair_list(count):
    return [(source, target) for source in range(count) for target in range(source, count)]


def reference(inputs, targets, enc_weight, enc_bias, dec_weight, dec_bias):
    pairs = pair_list(LAYERS)
    pre = [jnp.dot(inputs[s], enc_weight[s], preferred_element_type=jnp.float32) + enc_bias[s] for s in range(LAYERS)]
    acts = [jnp.maximum(value, 0.0).astype(jnp.bfloat16) for value in pre]
    errors = []
    for target in range(LAYERS):
        total = jnp.zeros((TOKENS, D), jnp.float32) + dec_bias[target].astype(jnp.float32)
        for index, (source, later) in enumerate(pairs):
            if later == target:
                total = total + jnp.dot(acts[source], dec_weight[index], preferred_element_type=jnp.float32)
        errors.append(total - targets[:, target, :].astype(jnp.float32))
    dec_bias_grad = jnp.stack([jnp.sum(value, axis=0) for value in errors]) / TOKENS
    derr = [(value / TOKENS).astype(jnp.bfloat16) for value in errors]
    dec_grad = jnp.stack([jnp.dot(acts[s].T, derr[t], preferred_element_type=jnp.float32) for (s, t) in pairs]).astype(jnp.bfloat16)
    enc_grads = []
    bias_grads = []
    for source in range(LAYERS):
        dacts = jnp.zeros((TOKENS, FEATS), jnp.float32)
        for index, (first, target) in enumerate(pairs):
            if first == source:
                dacts = dacts + jnp.dot(derr[target], dec_weight[index].T, preferred_element_type=jnp.float32)
        dpre = jnp.where(pre[source] > 0, dacts, jnp.zeros_like(dacts))
        bias_grads.append(jnp.sum(dpre, axis=0))
        enc_grads.append(jnp.dot(inputs[source].T, dpre.astype(jnp.bfloat16), preferred_element_type=jnp.float32).astype(jnp.bfloat16))
    return jnp.stack(enc_grads), jnp.stack(bias_grads), dec_grad, dec_bias_grad
```

```python
import jax
import jax.numpy as jnp
from jax import lax
from jax.experimental import pallas as pl
from jax.experimental.pallas import tpu as pltpu
from jax.sharding import Mesh
from jax.sharding import PartitionSpec as P

X, Y, C, Z, G = ("feat_0", "feat_1", "feat_2", "layer", "grp")
FEAT = (X, Y, C)
GRP_FEAT = (G, X, Y, C)
BF16, F32 = (jnp.bfloat16, jnp.float32)
VMEM = pl.BlockSpec(memory_space=pltpu.VMEM)
SMEM = pl.BlockSpec(memory_space=pltpu.SMEM)


def from_offset(x, axis, offset):
    size = lax.axis_size(axis)
    return lax.ppermute(x, axis, [((i + offset) % size, i) for i in range(size)])


def to_offset(x, axis, offset):
    return from_offset(x, axis, -offset)


def call(body, outs, args, scratch=(), flops=0, scalars=0, limit=56):
    moved = sum(a.size * a.dtype.itemsize for a in args)
    for shape, dtype in outs:
        count = 1
        for n in shape:
            count *= n
        moved += count * jnp.dtype(dtype).itemsize
    return pl.pallas_call(
        body,
        out_shape=[jax.ShapeDtypeStruct(s, d) for s, d in outs],
        in_specs=[SMEM] * scalars + [VMEM] * (len(args) - scalars),
        out_specs=[VMEM] * len(outs),
        scratch_shapes=list(scratch),
        cost_estimate=pl.CostEstimate(flops=flops, bytes_accessed=moved, transcendentals=0),
        compiler_params=pltpu.CompilerParams(vmem_limit_bytes=limit << 20),
    )(*args)


def lay_rows(parts, target):
    at = 0
    for part in parts:
        target[at : at + part.shape[0], :] = part[...]
        at += part.shape[0]


def encode(blocks, weight, bias):
    rows = sum(b.shape[0] for b in blocks)
    width, feats = weight.shape
    n = len(blocks)

    def body(*refs):
        parts, (w, b, joined, first, second, mask) = refs[:n], refs[n:]
        lay_rows(parts, joined)
        pre = jnp.dot(joined[...], w[...], preferred_element_type=F32) + b[...]
        acts = jnp.maximum(pre, 0.0).astype(BF16)
        first[...] = acts[: rows // 2]
        second[...] = acts[rows // 2 :]
        mask[...] = jnp.where(pre > 0, 1.0, 0.0).astype(BF16)

    half = ((rows // 2, feats), BF16)
    return call(
        body,
        [((rows, width), BF16), half, half, ((rows, feats), BF16)],
        [*blocks, weight, bias],
        flops=2 * rows * width * feats,
    )


def fresh(x, edge):
    lane = lax.broadcasted_iota(jnp.int32, x.shape, 1)
    return jnp.where(lane >= edge, x, jnp.zeros_like(x))


def nt(a, b):
    return lax.dot_general(a, b, (((1,), (1,)), ((), ())), preferred_element_type=F32)


def nn(a, b):
    return jnp.dot(a, b, preferred_element_type=F32)


def decode(here, sources, weight, block):
    half, feats = sources[0][0].shape
    rows = 2 * half
    d = block
    wide = 4 * d
    e = d % 128

    def body(here_ref, *refs):
        acts_in, (w, acts, keep, send) = refs[:8], refs[8:]
        for step in range(4):
            layer = lax.rem(here_ref[0] + step, 4)
            acts[layer, :half, :] = acts_in[2 * step][...]
            acts[layer, half:, :] = acts_in[2 * step + 1][...]
        for at, out in ((half, send), (0, keep)):
            a = [acts[s, at : at + half, :] for s in range(4)]
            out[:, : d - e] = nt(a[0], w[: d - e, :]).astype(BF16)
            part = nt(a[0], w[d - e : 2 * d, :]) + fresh(nt(a[1], w[4 * d - e : 5 * d, :]), e)
            out[:, d - e : 2 * d] = part.astype(BF16)
            part = (
                nt(a[0], w[2 * d : 3 * d - e, :])
                + nt(a[1], w[5 * d : 6 * d - e, :])
                + nt(a[2], w[7 * d : 8 * d - e, :])
            )
            out[:, 2 * d : 3 * d - e] = part.astype(BF16)
            part = (
                nt(a[0], w[3 * d - e : 4 * d, :])
                + nt(a[1], w[6 * d - e : 7 * d, :])
                + nt(a[2], w[8 * d - e : 9 * d, :])
                + fresh(nt(a[3], w[9 * d - e :, :]), e)
            )
            out[:, 3 * d - e :] = part.astype(BF16)

    return call(
        body,
        [((4, rows, feats), BF16), ((half, wide), BF16), ((half, wide), BF16)],
        [here, *[x for pair in sources for x in pair], weight],
        flops=20 * rows * feats * d,
        scalars=1,
    )


def feature_grads(here, blocks, weight, block):
    rows = sum(b.shape[0] for b in blocks)
    feats = weight.shape[1]
    d = block
    e = d % 128
    half = rows // 2
    n = len(blocks)

    def body(here_ref, *refs):
        parts, w, joined, outs, held = refs[:n], refs[n], refs[n + 1], refs[n + 2 : n + 10], refs[n + 10]
        lay_rows(parts, joined)

        def slot(layer):
            return lax.rem(layer + 4 - here_ref[0], 4)

        x = joined[...]
        held[slot(0)] = nn(x, w[: 4 * d, :]).astype(BF16)
        part = jnp.concatenate([fresh(x[:, d - e : d - e + 128], e), x[:, d - e + 128 :]], axis=1)
        held[slot(1)] = nn(part, w[4 * d - e : 7 * d, :]).astype(BF16)
        held[slot(2)] = nn(x[:, 2 * d :], w[7 * d : 9 * d, :]).astype(BF16)
        part = jnp.concatenate([fresh(x[:, 3 * d - e : 3 * d - e + 128], e), x[:, 3 * d - e + 128 :]], axis=1)
        held[slot(3)] = nn(part, w[9 * d - e :, :]).astype(BF16)
        for step in range(4):
            outs[2 * step][...] = held[step, :half, :]
            outs[2 * step + 1][...] = held[step, half:, :]

    res = call(
        body,
        [((rows, 4 * d), BF16)] + [((half, feats), BF16)] * 8,
        [here, *blocks, weight],
        scratch=[pltpu.VMEM((4, rows, feats), BF16)],
        flops=20 * rows * feats * d,
        scalars=1,
    )
    return res[0], res[1:]


def decoder_terms(acts, errors, block):
    _, rows, feats = acts[0].shape
    d = block
    e = d % 128
    n = len(acts)

    def body(*refs):
        a, x, out, turned = refs[:n], refs[n : 2 * n], refs[2 * n], refs[2 * n + 1]
        for k in range(n):
            turned[:, k * rows : (k + 1) * rows] = x[k][...].T
        at = 0
        for s in range(4):
            both = jnp.concatenate([a[k][s] for k in range(n)], axis=0)
            for t in range(s, 4):
                out[at : at + d, :] = nn(turned[t * d : (t + 1) * d, :], both).astype(BF16)
                at += d

    return call(
        body,
        [((10 * d, feats), BF16)],
        [*acts, *errors],
        scratch=[pltpu.VMEM((4 * d, n * rows), BF16)],
        flops=20 * n * rows * feats * d,
    )[0]


def gather_rows(block):
    half = block.shape[0] // 2
    x1 = from_offset(block, X, 1)
    y1 = from_offset(block, Y, 1)
    y3 = from_offset(block, Y, -1)
    near = jnp.concatenate([block, x1, y1, y3], axis=0)
    near_core = from_offset(near, C, 1)
    xy1 = from_offset(y1, X, 1)
    xy3 = from_offset(x1, Y, -1)
    y2 = from_offset(y1, Y, 1)
    xy2a = from_offset(xy1[:half], Y, 1)
    xy2b = from_offset(xy3[half:], Y, -1)
    far = jnp.concatenate([xy1, xy3, y2, xy2a, xy2b], axis=0)
    far_core = from_offset(far, C, 1)
    return [near, near_core], [far, far_core]


def sum_rows(near, far):
    rows = near[0].shape[0] // 4
    half = rows // 2
    near_in = from_offset(near[1], C, 1)
    far_in = from_offset(far[1], C, 1)

    def taken(pair, arrived, k):
        cut = slice(k * rows, (k + 1) * rows)
        return pair[cut].astype(F32) + arrived[cut].astype(F32)

    q00, q10, q01, q03 = [taken(near[0], near_in, k) for k in range(4)]
    q11, q13, q02, q12 = [taken(far[0], far_in, k) for k in range(4)]
    r03 = to_offset(q03.astype(BF16), Y, -1)
    a = to_offset(q12[:half].astype(BF16), Y, 1).astype(F32)
    b = to_offset(q12[half:].astype(BF16), Y, -1).astype(F32)
    r02 = to_offset(q02.astype(BF16), Y, 1)
    q11 = jnp.concatenate([q11[:half] + a, q11[half:]], axis=0)
    q13 = jnp.concatenate([q13[:half], q13[half:] + b], axis=0)
    r11 = to_offset(q11.astype(BF16), X, 1)
    r13 = to_offset(q13.astype(BF16), Y, -1)
    q01 = q01 + r11.astype(F32) + r02.astype(F32)
    q10 = q10 + r13.astype(F32)
    r01 = to_offset(q01.astype(BF16), Y, 1)
    r10 = to_offset(q10.astype(BF16), X, 1)
    return q00 + r03.astype(F32) + r01.astype(F32) + r10.astype(F32)


def gather_layers(first, second):
    a1 = from_offset(first, Z, 1)
    b3 = from_offset(second, Z, -1)
    b1 = from_offset(second, Z, 1)
    a3 = from_offset(first, Z, -1)
    a2 = from_offset(a1, Z, 1)
    b2 = from_offset(b3, Z, -1)
    return [(first, second), (a1, b1), (a2, b2), (a3, b3)]


def sum_layers(parts):
    a0, b0, a1, b1, a2, b2, a3, b3 = parts
    a2 = to_offset(a2, Z, 1)
    b2 = to_offset(b2, Z, -1)
    b1 = to_offset(b1, Z, 1)
    a3 = to_offset(a3, Z, -1)
    a1 = to_offset((a1.astype(F32) + a2.astype(F32)).astype(BF16), Z, 1)
    b3 = to_offset((b3.astype(F32) + b2.astype(F32)).astype(BF16), Z, -1)
    first = a0.astype(F32) + a1.astype(F32) + a3.astype(F32)
    second = b0.astype(F32) + b1.astype(F32) + b3.astype(F32)
    return jnp.concatenate([first, second], axis=0)


def exchanged(x):
    own = lax.axis_index(G)
    half = x.shape[0] // 2
    sent = lax.dynamic_slice_in_dim(x, (1 - own) * half, half, 0)
    kept = lax.dynamic_slice_in_dim(x, own * half, half, 0)
    arrived = from_offset(sent, G, 1)
    return (kept.astype(F32) + arrived.astype(F32)).astype(x.dtype)


def per_device(inputs, targets, enc_weight, enc_bias, dec_weight, dec_bias):
    layers, d = dec_bias.shape
    here = lax.axis_index(Z).astype(jnp.int32)[None]
    tok_dev = inputs.shape[1]
    total_tokens = tok_dev * lax.axis_size(FEAT) * lax.axis_size(G)
    feats = dec_weight.shape[1]
    decoder = dec_weight.transpose(0, 2, 1).reshape(-1, feats)
    wanted = targets.astype(F32).reshape(tok_dev, -1) - dec_bias.reshape(1, -1)

    chunks = gather_rows(inputs[0])
    rows, masks, acts, partial = [], [], [], []
    for chunk in chunks:
        joined, first, second, mask = encode(chunk, enc_weight[0], enc_bias)
        rows.append(joined)
        masks.append(mask)
        a, keep, send = decode(here, gather_layers(first, second), decoder, d)
        acts.append(a)
        partial.append((keep, send))
    errors = sum_rows(*partial) - wanted
    dec_bias_grad = lax.psum(jnp.sum(errors, axis=0), GRP_FEAT) / total_tokens
    scaled = (errors / total_tokens).astype(BF16)

    derr, dpre = [], []
    for chunk, mask in zip(gather_rows(scaled), masks):
        joined, parts = feature_grads(here, chunk, decoder, d)
        derr.append(joined)
        dacts = sum_layers(parts)
        dpre.append(jnp.where(mask > 0, dacts, jnp.zeros_like(dacts)))
    dec_grad = exchanged(decoder_terms(acts, derr, d))
    enc_bias_grad = sum(jnp.sum(x, axis=0) for x in dpre)
    enc_bias_grad = enc_bias_grad + from_offset(enc_bias_grad, G, 1)
    enc_grad = sum(
        jnp.einsum("rd,rf->df", r, x.astype(BF16), preferred_element_type=F32) for r, x in zip(rows, dpre)
    )
    enc_grad = exchanged(enc_grad.astype(BF16))
    return (
        enc_grad[None],
        enc_bias_grad[None],
        dec_grad.reshape(-1, d, feats).transpose(0, 2, 1),
        dec_bias_grad.reshape(layers, d),
    )


def solution(mesh):
    finer = Mesh(
        mesh.devices.reshape(mesh.shape["grp"], mesh.shape["layer"], 2, 4, 2),
        (G, Z, X, Y, C),
    )
    return jax.shard_map(
        per_device,
        mesh=finer,
        in_specs=(
            P(Z, GRP_FEAT, None),
            P(GRP_FEAT, None, Z),
            P(Z, None, FEAT),
            P(Z, FEAT),
            P(None, FEAT, Z),
            P(None, Z),
        ),
        out_specs=(P(Z, G, FEAT), P(Z, FEAT), P(G, FEAT, Z), P(None, Z)),
        check_vma=False,
    )
```

```python
import jax
import jax.numpy as jnp
from jax import lax
from jax.experimental import pallas as pl
from jax.experimental.pallas import tpu as pltpu
from jax.sharding import Mesh
from jax.sharding import PartitionSpec as P

X, Y, C, Z, G = ("feat_0", "feat_1", "feat_2", "layer", "grp")
FEAT = (X, Y, C)
GRP_FEAT = (G, X, Y, C)
BF16, F32 = (jnp.bfloat16, jnp.float32)
VMEM = pl.BlockSpec(memory_space=pltpu.VMEM)
SMEM = pl.BlockSpec(memory_space=pltpu.SMEM)


def from_offset(x, axis, offset):
    size = lax.axis_size(axis)
    return lax.ppermute(x, axis, [((i + offset) % size, i) for i in range(size)])


def to_offset(x, axis, offset):
    return from_offset(x, axis, -offset)


def after(x, earlier):
    return lax.optimization_barrier((x, earlier))[0]


def size_of(shape, dtype):
    count = jnp.dtype(dtype).itemsize
    for n in shape:
        count *= n
    return count


def call(body, outs, place, args, scratch=(), flops=0):
    moved = sum(size_of(a.shape, a.dtype) for a in args) + sum(size_of(*o) for o in outs)
    held = moved + sum(size_of(*s) for s in scratch)
    return pl.pallas_call(
        body,
        out_shape=[jax.ShapeDtypeStruct(s, d) for s, d in outs],
        in_specs=[SMEM] + [VMEM] * len(args),
        out_specs=[VMEM] * len(outs),
        scratch_shapes=[pltpu.VMEM(s, d) for s, d in scratch],
        cost_estimate=pl.CostEstimate(flops=flops, bytes_accessed=moved, transcendentals=0),
        compiler_params=pltpu.CompilerParams(vmem_limit_bytes=held + (4 << 20)),
    )(place, *args)


def lay_rows(parts, target):
    at = 0
    for part in parts:
        target[at : at + part.shape[0], :] = part[...]
        at += part.shape[0]


def encode(place, blocks, weight, bias):
    rows = sum(b.shape[0] for b in blocks)
    width, feats = weight.shape
    n = len(blocks)

    def body(_, *refs):
        parts, (w, b, joined, acts, mask) = refs[:n], refs[n:]
        lay_rows(parts, joined)
        pre = jnp.dot(joined[...], w[...], preferred_element_type=F32) + b[...]
        acts[...] = jnp.maximum(pre, 0.0).astype(BF16)
        mask[...] = jnp.where(pre > 0, 1.0, 0.0).astype(BF16)

    return call(
        body,
        [((rows, width), BF16), ((rows, feats), BF16), ((rows, feats), BF16)],
        place,
        [*blocks, weight, bias],
        flops=2 * rows * width * feats,
    )


def fresh(x, edge):
    lane = lax.broadcasted_iota(jnp.int32, x.shape, 1)
    return jnp.where(lane >= edge, x, jnp.zeros_like(x))


def nt(a, b):
    return lax.dot_general(a, b, (((1,), (1,)), ((), ())), preferred_element_type=F32)


def nn(a, b):
    return jnp.dot(a, b, preferred_element_type=F32)


def decode(place, sources, weight, block):
    rows, feats = sources[0].shape
    half = rows // 2
    d = block
    wide = 4 * d
    e = d % 128

    def body(at_ref, *refs):
        a0, a1, a3, a2, b2, w, acts, keep, send = refs
        for step, part in ((0, a0), (1, a1), (3, a3)):
            acts[lax.rem(at_ref[0] + step, 4)] = part[...]
        layer = lax.rem(at_ref[0] + 2, 4)
        acts[layer, :half, :] = a2[...]
        acts[layer, half:, :] = b2[...]
        for at, out in ((half, send), (0, keep)):
            a = [acts[s, at : at + half, :] for s in range(4)]
            out[:, : d - e] = nt(a[0], w[: d - e, :]).astype(BF16)
            part = nt(a[0], w[d - e : 2 * d, :]) + fresh(nt(a[1], w[4 * d - e : 5 * d, :]), e)
            out[:, d - e : 2 * d] = part.astype(BF16)
            part = (
                nt(a[0], w[2 * d : 3 * d - e, :])
                + nt(a[1], w[5 * d : 6 * d - e, :])
                + nt(a[2], w[7 * d : 8 * d - e, :])
            )
            out[:, 2 * d : 3 * d - e] = part.astype(BF16)
            part = (
                nt(a[0], w[3 * d - e : 4 * d, :])
                + nt(a[1], w[6 * d - e : 7 * d, :])
                + nt(a[2], w[8 * d - e : 9 * d, :])
                + fresh(nt(a[3], w[9 * d - e :, :]), e)
            )
            out[:, 3 * d - e :] = part.astype(BF16)

    return call(
        body,
        [((4, rows, feats), BF16), ((half, wide), BF16), ((half, wide), BF16)],
        place,
        [*sources, weight],
        flops=20 * rows * feats * d,
    )


def feature_grads(place, blocks, weight, block):
    rows = sum(b.shape[0] for b in blocks)
    feats = weight.shape[1]
    d = block
    e = d % 128
    half = rows // 2
    n = len(blocks)

    def body(at_ref, *refs):
        parts, (w, own, up, down, a1, b3, held, joined) = refs[:n], refs[n:]
        lay_rows(parts, joined)

        def slot(layer):
            return lax.rem(layer + 4 - at_ref[0], 4)

        x = joined[...]
        held[slot(0)] = nn(x, w[: 4 * d, :]).astype(BF16)
        part = jnp.concatenate([fresh(x[:, d - e : d - e + 128], e), x[:, d - e + 128 :]], axis=1)
        held[slot(1)] = nn(part, w[4 * d - e : 7 * d, :]).astype(BF16)
        held[slot(2)] = nn(x[:, 2 * d :], w[7 * d : 9 * d, :]).astype(BF16)
        part = jnp.concatenate([fresh(x[:, 3 * d - e : 3 * d - e + 128], e), x[:, 3 * d - e + 128 :]], axis=1)
        held[slot(3)] = nn(part, w[9 * d - e :, :]).astype(BF16)
        own[...] = held[0]
        up[:half, :] = held[2, :half, :]
        up[half:, :] = held[1, half:, :]
        down[:half, :] = held[3, :half, :]
        down[half:, :] = held[2, half:, :]
        a1[...] = held[1, :half, :]
        b3[...] = held[3, half:, :]

    return call(
        body,
        [((rows, feats), BF16)] * 3 + [((half, feats), BF16)] * 2,
        place,
        [*blocks, weight],
        scratch=[((4, rows, feats), BF16), ((rows, 4 * d), BF16)],
        flops=20 * rows * feats * d,
    )


NEAR = ((0, 0), (1, 0), (0, 1), (0, 3))
FAR = ((1, 1), (1, 3), (0, 2), (1, 2))
PAIRS = tuple((s, t) for s in range(4) for t in range(s, 4))


def own_pairs_grad(place, acts, errors, other_acts, other_errors, block):
    _, rows, feats = acts[0].shape
    d = block
    wide = 4 * d
    tokens = other_errors.shape[1]
    count = 4 * rows
    own = len(PAIRS) // 2

    def body(at_ref, a0, a1, x0, x1, x2, x3, a2, others, out, total, turned, laid):
        at = 0
        for blocks in (NEAR, FAR):
            for core in range(2):
                for dx, dy in blocks:
                    x = lax.rem(at_ref[2] + dx, 2)
                    y = lax.rem(at_ref[3] + dy, 4)
                    c = lax.rem(at_ref[4] + core, 2)
                    laid[at : at + tokens, :] = others[(x * 4 + y) * 2 + c]
                    at += tokens
        sums = jnp.zeros((8, wide), F32)
        at = 0
        for part in (x0, x1, x2, x3, laid):
            x = part[...]
            size = x.shape[0]
            sums += nn(jnp.ones((8, size), BF16), x)
            for t in range(4):
                low = t * d // 128 * 128
                turned[t, :, at : at + size] = x[:, low : (t + 1) * d].T[t * d - low :]
            at += size
        total[...] = sums
        first = at_ref[1] == 0
        for i in range(own):
            s, t = [jnp.where(first, m, n) for m, n in zip(PAIRS[i], PAIRS[own + i])]
            part = nn(turned[t, :, :rows], a0[s]) + nn(turned[t, :, rows : 2 * rows], a1[s])
            out[i] = (part + nn(turned[t, :, 2 * rows :], a2[s])).astype(BF16)

    return call(
        body,
        [((own, d, feats), BF16), ((8, wide), F32)],
        place,
        [*acts, *errors, other_acts, other_errors],
        scratch=[((4, d, count), BF16), ((2 * rows, wide), BF16)],
        flops=10 * count * feats * d,
    )


def gather_rows(block, use):
    half = block.shape[0] // 2
    x1 = from_offset(block, X, 1)
    y1 = from_offset(block, Y, 1)
    y3 = from_offset(block, Y, -1)
    near = jnp.concatenate([block, x1, y1, y3], axis=0)
    xy1 = from_offset(y1, X, 1)
    xy3 = from_offset(x1, Y, -1)
    y2 = from_offset(y1, Y, 1)
    xy1, xy3 = after((xy1, xy3), near)
    near_core = from_offset(near, C, 1)
    xy2a = from_offset(xy1[:half], Y, 1)
    xy2b = from_offset(xy3[half:], Y, -1)
    first, (made, arrived) = use([near, near_core])
    far = jnp.concatenate(after([xy1, xy3, y2, xy2a, xy2b], made), axis=0)
    far_core = after(from_offset(far, C, 1), arrived)
    return first, use([far, far_core])[0]


def sum_rows(near, far):
    rows = near[0].shape[0] // 4
    half = rows // 2
    near_in = from_offset(near[1], C, 1)
    far_in = from_offset(far[1], C, 1)

    def taken(pair, arrived, k):
        cut = slice(k * rows, (k + 1) * rows)
        return pair[cut].astype(F32) + arrived[cut].astype(F32)

    q00, q10, q01, q03 = [taken(near[0], near_in, k) for k in range(4)]
    q11, q13, q02, q12 = [taken(far[0], far_in, k) for k in range(4)]
    r03 = to_offset(q03.astype(BF16), Y, -1)
    a = to_offset(q12[:half].astype(BF16), Y, 1).astype(F32)
    b = to_offset(q12[half:].astype(BF16), Y, -1).astype(F32)
    r02 = to_offset(q02.astype(BF16), Y, 1)
    q11 = jnp.concatenate([q11[:half] + a, q11[half:]], axis=0)
    q13 = jnp.concatenate([q13[:half], q13[half:] + b], axis=0)
    r11 = to_offset(q11.astype(BF16), X, 1)
    r13 = to_offset(q13.astype(BF16), Y, -1)
    q01 = q01 + r11.astype(F32) + r02.astype(F32)
    q10 = q10 + r13.astype(F32)
    r01 = to_offset(q01.astype(BF16), Y, 1)
    r10 = to_offset(q10.astype(BF16), X, 1)
    return q00 + r03.astype(F32) + r01.astype(F32) + r10.astype(F32)


def gather_layers(acts, earlier):
    half = acts.shape[0] // 2
    a1 = from_offset(acts, Z, 1)
    a3 = from_offset(acts, Z, -1)
    gate = (a1, a3)
    a1, a3 = after((a1, a3), earlier)
    a2 = from_offset(a1[:half], Z, 1)
    b2 = from_offset(a3[half:], Z, -1)
    return (acts, a1, a3, a2, b2), gate


def sum_layers(own, up, down, a1, b3):
    half = a1.shape[0]
    up = to_offset(up, Z, 1)
    down = to_offset(down, Z, -1)
    gate = (up, down)
    a1 = to_offset((a1.astype(F32) + up[:half].astype(F32)).astype(BF16), Z, 1)
    b3 = to_offset((b3.astype(F32) + down[half:].astype(F32)).astype(BF16), Z, -1)
    first = own[:half].astype(F32) + a1.astype(F32) + down[:half].astype(F32)
    second = own[half:].astype(F32) + up[half:].astype(F32) + b3.astype(F32)
    return jnp.concatenate([first, second], axis=0), gate


def exchanged(x, meanwhile):
    own = lax.axis_index(G)
    half = x.shape[0] // 2
    sent = lax.dynamic_slice_in_dim(x, (1 - own) * half, half, 0)
    kept = lax.dynamic_slice_in_dim(x, own * half, half, 0)
    arrived = after(from_offset(sent, G, 1), meanwhile(sent))
    return (kept.astype(F32) + arrived.astype(F32)).astype(x.dtype)


def per_device(inputs, targets, enc_weight, enc_bias, dec_weight, dec_bias):
    layers, d = dec_bias.shape
    place = jnp.stack([lax.axis_index(axis) for axis in (Z, G, X, Y, C)]).astype(jnp.int32)
    tok_dev = inputs.shape[1]
    total_tokens = tok_dev * lax.axis_size(FEAT) * lax.axis_size(G)
    feats = dec_weight.shape[1]
    decoder = dec_weight.transpose(0, 2, 1).reshape(-1, feats)
    wanted = targets.astype(F32).reshape(tok_dev, -1) - dec_bias.reshape(1, -1)

    second_hops = []

    def forward(chunk):
        joined, acts, mask = encode(place, chunk, enc_weight[0], enc_bias)
        sources, gate = gather_layers(acts, tuple(second_hops))
        second_hops.extend(sources[3:])
        return (joined, mask, sources, gate), (acts, gate)

    near, far = gather_rows(inputs[0], forward)
    other_acts = from_offset(jnp.concatenate([near[2][0], far[2][0]], axis=0), G, 1)
    acts, keep, send = decode(place, after(near[2], far[3]), decoder, d)
    acts, partial = [acts], [(keep, send)]
    far_sources = after(far[2], (keep, other_acts))
    far_acts, keep, send = decode(place, far_sources, decoder, d)
    acts.append(far_acts)
    partial.append((keep, send))
    errors = sum_rows(*partial) - wanted
    other_acts = lax.all_gather(other_acts, Z, axis=0)
    scaled = (errors / total_tokens).astype(BF16)

    def backward(chunk):
        parts = feature_grads(place, chunk, decoder, d)
        dacts, gate = sum_layers(*parts)
        return (chunk, dacts, parts[0]), (parts[0], gate)

    other_errors = from_offset(scaled, G, 1)
    graded = gather_rows(scaled, backward)
    other_errors = lax.all_gather(after(other_errors, graded[1][2]), FEAT, axis=0)
    dpre = [jnp.where(c[1] > 0, g[1], jnp.zeros_like(g[1])) for c, g in zip((near, far), graded)]
    enc_bias_grad = sum(jnp.sum(x, axis=0) for x in dpre)
    enc_bias_grad = enc_bias_grad + from_offset(enc_bias_grad, G, 1)
    enc_grad = sum(
        jnp.einsum("rd,rf->df", chunk[0], x.astype(BF16), preferred_element_type=F32)
        for chunk, x in zip((near, far), dpre)
    )
    made = []

    def meanwhile(sent):
        errors_in = after(other_errors, sent)
        made.extend(own_pairs_grad(place, acts, [*graded[0][0], *graded[1][0]], other_acts, errors_in, d))
        return made[0]

    enc_grad = exchanged(enc_grad.astype(BF16), meanwhile)
    dec_grad, error_sums = made
    return (
        enc_grad[None],
        enc_bias_grad[None],
        dec_grad.transpose(0, 2, 1),
        error_sums[0].reshape(layers, d),
    )


def solution(mesh):
    finer = Mesh(
        mesh.devices.reshape(mesh.shape["grp"], mesh.shape["layer"], 2, 4, 2),
        (G, Z, X, Y, C),
    )
    return jax.shard_map(
        per_device,
        mesh=finer,
        in_specs=(
            P(Z, GRP_FEAT, None),
            P(GRP_FEAT, None, Z),
            P(Z, None, FEAT),
            P(Z, FEAT),
            P(None, FEAT, Z),
            P(None, Z),
        ),
        out_specs=(P(Z, G, FEAT), P(Z, FEAT), P(G, FEAT, Z), P(None, Z)),
        check_vma=False,
    )
```

```python
import jax
import jax.numpy as jnp
from jax import lax
from jax.experimental import pallas as pl
from jax.experimental.pallas import tpu as pltpu
from jax.sharding import Mesh
from jax.sharding import PartitionSpec as P

X, Y, C, Z, G = ("feat_0", "feat_1", "feat_2", "layer", "grp")
FEAT = (X, Y, C)
GRP_FEAT = (G, X, Y, C)
BF16, F32 = (jnp.bfloat16, jnp.float32)
VMEM = pl.BlockSpec(memory_space=pltpu.VMEM)
SMEM = pl.BlockSpec(memory_space=pltpu.SMEM)


def from_offset(x, axis, offset):
    size = lax.axis_size(axis)
    return lax.ppermute(x, axis, [((i + offset) % size, i) for i in range(size)])


def to_offset(x, axis, offset):
    return from_offset(x, axis, -offset)


def after(x, earlier):
    return lax.optimization_barrier((x, earlier))[0]


def size_of(shape, dtype):
    count = jnp.dtype(dtype).itemsize
    for n in shape:
        count *= n
    return count


def call(body, outs, place, args, scratch=(), flops=0):
    moved = sum(size_of(a.shape, a.dtype) for a in args) + sum(size_of(*o) for o in outs)
    held = moved + sum(size_of(*s) for s in scratch)
    return pl.pallas_call(
        body,
        out_shape=[jax.ShapeDtypeStruct(s, d) for s, d in outs],
        in_specs=[SMEM] + [VMEM] * len(args),
        out_specs=[VMEM] * len(outs),
        scratch_shapes=[pltpu.VMEM(s, d) for s, d in scratch],
        cost_estimate=pl.CostEstimate(flops=flops, bytes_accessed=moved, transcendentals=0),
        compiler_params=pltpu.CompilerParams(vmem_limit_bytes=held + (4 << 20)),
    )(place, *args)


def lay_rows(parts, target):
    at = 0
    for part in parts:
        target[at : at + part.shape[0], :] = part[...]
        at += part.shape[0]


def encode(place, blocks, weight, bias):
    rows = sum(b.shape[0] for b in blocks)
    width, feats = weight.shape
    n = len(blocks)

    def body(_, *refs):
        parts, (w, b, joined, acts, mask) = refs[:n], refs[n:]
        lay_rows(parts, joined)
        pre = jnp.dot(joined[...], w[...], preferred_element_type=F32) + b[...]
        acts[...] = jnp.maximum(pre, 0.0).astype(BF16)
        mask[...] = jnp.where(pre > 0, 1.0, 0.0).astype(BF16)

    return call(
        body,
        [((rows, width), BF16), ((rows, feats), BF16), ((rows, feats), BF16)],
        place,
        [*blocks, weight, bias],
        flops=2 * rows * width * feats,
    )


def fresh(x, edge):
    lane = lax.broadcasted_iota(jnp.int32, x.shape, 1)
    return jnp.where(lane >= edge, x, jnp.zeros_like(x))


def nt(a, b):
    return lax.dot_general(a, b, (((1,), (1,)), ((), ())), preferred_element_type=F32)


def nn(a, b):
    return jnp.dot(a, b, preferred_element_type=F32)


def decode(place, sources, weight, block):
    rows, feats = sources[0].shape
    half = rows // 2
    d = block
    wide = 4 * d
    e = d % 128

    def body(at_ref, *refs):
        a0, a1, a3, a2, b2, w, acts, keep, send = refs
        for step, part in ((0, a0), (1, a1), (3, a3)):
            acts[lax.rem(at_ref[0] + step, 4)] = part[...]
        layer = lax.rem(at_ref[0] + 2, 4)
        acts[layer, :half, :] = a2[...]
        acts[layer, half:, :] = b2[...]
        for at, out in ((half, send), (0, keep)):
            a = [acts[s, at : at + half, :] for s in range(4)]
            out[:, : d - e] = nt(a[0], w[: d - e, :]).astype(BF16)
            part = nt(a[0], w[d - e : 2 * d, :]) + fresh(nt(a[1], w[4 * d - e : 5 * d, :]), e)
            out[:, d - e : 2 * d] = part.astype(BF16)
            part = (
                nt(a[0], w[2 * d : 3 * d - e, :])
                + nt(a[1], w[5 * d : 6 * d - e, :])
                + nt(a[2], w[7 * d : 8 * d - e, :])
            )
            out[:, 2 * d : 3 * d - e] = part.astype(BF16)
            part = (
                nt(a[0], w[3 * d - e : 4 * d, :])
                + nt(a[1], w[6 * d - e : 7 * d, :])
                + nt(a[2], w[8 * d - e : 9 * d, :])
                + fresh(nt(a[3], w[9 * d - e :, :]), e)
            )
            out[:, 3 * d - e :] = part.astype(BF16)

    return call(
        body,
        [((4, rows, feats), BF16), ((half, wide), BF16), ((half, wide), BF16)],
        place,
        [*sources, weight],
        flops=20 * rows * feats * d,
    )


def feature_grads(place, blocks, weight, block):
    rows = sum(b.shape[0] for b in blocks)
    feats = weight.shape[1]
    d = block
    e = d % 128
    half = rows // 2
    n = len(blocks)

    def body(at_ref, *refs):
        parts, (w, own, up, down, a1, b3, held, joined) = refs[:n], refs[n:]
        lay_rows(parts, joined)

        def slot(layer):
            return lax.rem(layer + 4 - at_ref[0], 4)

        x = joined[...]
        held[slot(0)] = nn(x, w[: 4 * d, :]).astype(BF16)
        part = jnp.concatenate([fresh(x[:, d - e : d - e + 128], e), x[:, d - e + 128 :]], axis=1)
        held[slot(1)] = nn(part, w[4 * d - e : 7 * d, :]).astype(BF16)
        held[slot(2)] = nn(x[:, 2 * d :], w[7 * d : 9 * d, :]).astype(BF16)
        part = jnp.concatenate([fresh(x[:, 3 * d - e : 3 * d - e + 128], e), x[:, 3 * d - e + 128 :]], axis=1)
        held[slot(3)] = nn(part, w[9 * d - e :, :]).astype(BF16)
        own[...] = held[0]
        up[:half, :] = held[2, :half, :]
        up[half:, :] = held[1, half:, :]
        down[:half, :] = held[3, :half, :]
        down[half:, :] = held[2, half:, :]
        a1[...] = held[1, :half, :]
        b3[...] = held[3, half:, :]

    return call(
        body,
        [((rows, feats), BF16)] * 3 + [((half, feats), BF16)] * 2,
        place,
        [*blocks, weight],
        scratch=[((4, rows, feats), BF16), ((rows, 4 * d), BF16)],
        flops=20 * rows * feats * d,
    )


NEAR = ((0, 0), (1, 0), (0, 1), (0, 3))
FAR = ((1, 1), (1, 3), (0, 2), (1, 2))
PAIRS = tuple((s, t) for s in range(4) for t in range(s, 4))


def own_pairs_grad(place, acts, errors, other_acts, other_errors, block):
    _, rows, feats = acts[0].shape
    d = block
    wide = 4 * d
    tokens = other_errors.shape[1]
    count = 4 * rows
    own = len(PAIRS) // 2

    def body(at_ref, a0, a1, x0, x1, x2, x3, a2, others, out, total, turned, laid):
        at = 0
        for blocks in (NEAR, FAR):
            for core in range(2):
                for dx, dy in blocks:
                    x = lax.rem(at_ref[2] + dx, 2)
                    y = lax.rem(at_ref[3] + dy, 4)
                    c = lax.rem(at_ref[4] + core, 2)
                    laid[at : at + tokens, :] = others[(x * 4 + y) * 2 + c]
                    at += tokens
        sums = jnp.zeros((8, wide), F32)
        at = 0
        for part in (x0, x1, x2, x3, laid):
            x = part[...]
            size = x.shape[0]
            sums += nn(jnp.ones((8, size), BF16), x)
            for t in range(4):
                low = t * d // 128 * 128
                turned[t, :, at : at + size] = x[:, low : (t + 1) * d].T[t * d - low :]
            at += size
        total[...] = sums
        first = at_ref[1] == 0
        for i in range(own):
            s, t = [jnp.where(first, m, n) for m, n in zip(PAIRS[i], PAIRS[own + i])]
            part = nn(turned[t, :, :rows], a0[s]) + nn(turned[t, :, rows : 2 * rows], a1[s])
            out[i] = (part + nn(turned[t, :, 2 * rows :], a2[s])).astype(BF16)

    return call(
        body,
        [((own, d, feats), BF16), ((8, wide), F32)],
        place,
        [*acts, *errors, other_acts, other_errors],
        scratch=[((4, d, count), BF16), ((2 * rows, wide), BF16)],
        flops=10 * count * feats * d,
    )


def gather_rows(block, use):
    half = block.shape[0] // 2
    x1 = from_offset(block, X, 1)
    y1 = from_offset(block, Y, 1)
    y3 = from_offset(block, Y, -1)
    near = jnp.concatenate([block, x1, y1, y3], axis=0)
    xy1 = from_offset(y1, X, 1)
    xy3 = from_offset(x1, Y, -1)
    y2 = from_offset(y1, Y, 1)
    near_core = from_offset(near, C, 1)
    first, made = use([near, near_core])
    xy1, xy3 = after((xy1, xy3), made)
    xy2a = from_offset(xy1[:half], Y, 1)
    xy2b = from_offset(xy3[half:], Y, -1)
    far = jnp.concatenate([xy1, xy3, y2, xy2a, xy2b], axis=0)
    far_core = from_offset(far, C, 1)
    return first, use([far, far_core])[0]


def sum_rows(near, far):
    rows = near[0].shape[0] // 4
    half = rows // 2
    near_in = from_offset(near[1], C, 1)
    far_in = from_offset(far[1], C, 1)

    def taken(pair, arrived, k):
        cut = slice(k * rows, (k + 1) * rows)
        return pair[cut].astype(F32) + arrived[cut].astype(F32)

    q00, q10, q01, q03 = [taken(near[0], near_in, k) for k in range(4)]
    q11, q13, q02, q12 = [taken(far[0], far_in, k) for k in range(4)]
    r03 = to_offset(q03.astype(BF16), Y, -1)
    a = to_offset(q12[:half].astype(BF16), Y, 1).astype(F32)
    b = to_offset(q12[half:].astype(BF16), Y, -1).astype(F32)
    r02 = to_offset(q02.astype(BF16), Y, 1)
    q11 = jnp.concatenate([q11[:half] + a, q11[half:]], axis=0)
    q13 = jnp.concatenate([q13[:half], q13[half:] + b], axis=0)
    r11 = to_offset(q11.astype(BF16), X, 1)
    r13 = to_offset(q13.astype(BF16), Y, -1)
    q01 = q01 + r11.astype(F32) + r02.astype(F32)
    q10 = q10 + r13.astype(F32)
    r01 = to_offset(q01.astype(BF16), Y, 1)
    r10 = to_offset(q10.astype(BF16), X, 1)
    return q00 + r03.astype(F32) + r01.astype(F32) + r10.astype(F32)


def gather_layers(acts, earlier):
    half = acts.shape[0] // 2
    a1 = from_offset(acts, Z, 1)
    a3 = from_offset(acts, Z, -1)
    gate = (a1, a3)
    a1, a3 = after((a1, a3), earlier)
    a2 = from_offset(a1[:half], Z, 1)
    b2 = from_offset(a3[half:], Z, -1)
    return (acts, a1, a3, a2, b2), gate


def sum_layers(own, up, down, a1, b3):
    half = a1.shape[0]
    up = to_offset(up, Z, 1)
    down = to_offset(down, Z, -1)
    gate = (up, down)
    a1 = to_offset((a1.astype(F32) + up[:half].astype(F32)).astype(BF16), Z, 1)
    b3 = to_offset((b3.astype(F32) + down[half:].astype(F32)).astype(BF16), Z, -1)
    first = own[:half].astype(F32) + a1.astype(F32) + down[:half].astype(F32)
    second = own[half:].astype(F32) + up[half:].astype(F32) + b3.astype(F32)
    return jnp.concatenate([first, second], axis=0), gate


def exchanged(x, meanwhile):
    own = lax.axis_index(G)
    half = x.shape[0] // 2
    sent = lax.dynamic_slice_in_dim(x, (1 - own) * half, half, 0)
    kept = lax.dynamic_slice_in_dim(x, own * half, half, 0)
    arrived = after(from_offset(sent, G, 1), meanwhile(sent))
    return (kept.astype(F32) + arrived.astype(F32)).astype(x.dtype)


def per_device(inputs, targets, enc_weight, enc_bias, dec_weight, dec_bias):
    layers, d = dec_bias.shape
    place = jnp.stack([lax.axis_index(axis) for axis in (Z, G, X, Y, C)]).astype(jnp.int32)
    tok_dev = inputs.shape[1]
    total_tokens = tok_dev * lax.axis_size(FEAT) * lax.axis_size(G)
    feats = dec_weight.shape[1]
    decoder = dec_weight.transpose(0, 2, 1).reshape(-1, feats)
    wanted = targets.astype(F32).reshape(tok_dev, -1) - dec_bias.reshape(1, -1)

    second_hops = []

    def forward(chunk):
        joined, acts, mask = encode(place, chunk, enc_weight[0], enc_bias)
        sources, gate = gather_layers(acts, tuple(second_hops))
        second_hops.extend(sources[3:])
        return (joined, mask, sources, gate), acts

    near, far = gather_rows(inputs[0], forward)
    other_acts = from_offset(jnp.concatenate([near[2][0], far[2][0]], axis=0), G, 1)
    acts, keep, send = decode(place, after(near[2], far[3]), decoder, d)
    acts, partial = [acts], [(keep, send)]
    far_sources = after(far[2], (keep, other_acts))
    far_acts, keep, send = decode(place, far_sources, decoder, d)
    acts.append(far_acts)
    partial.append((keep, send))
    errors = sum_rows(*partial) - wanted
    other_acts = lax.all_gather(other_acts, Z, axis=0)
    scaled = (errors / total_tokens).astype(BF16)

    def backward(chunk):
        parts = feature_grads(place, chunk, decoder, d)
        dacts, gate = sum_layers(*parts)
        return (chunk, dacts, gate, parts[0]), parts[0]

    other_errors = from_offset(scaled, G, 1)
    graded = gather_rows(scaled, backward)
    other_errors = lax.all_gather(after(other_errors, (graded[0][2], graded[1][3], other_acts)), FEAT, axis=0)
    dpre = [jnp.where(c[1] > 0, g[1], jnp.zeros_like(g[1])) for c, g in zip((near, far), graded)]
    enc_bias_grad = sum(jnp.sum(x, axis=0) for x in dpre)
    enc_bias_grad = enc_bias_grad + from_offset(enc_bias_grad, G, 1)
    enc_grad = sum(
        jnp.einsum("rd,rf->df", chunk[0], x.astype(BF16), preferred_element_type=F32)
        for chunk, x in zip((near, far), dpre)
    )
    made = []

    def meanwhile(sent):
        errors_in = after(other_errors, sent)
        made.extend(own_pairs_grad(place, acts, [*graded[0][0], *graded[1][0]], other_acts, errors_in, d))
        return made[0]

    enc_grad = exchanged(enc_grad.astype(BF16), meanwhile)
    dec_grad, error_sums = made
    return (
        enc_grad[None],
        enc_bias_grad[None],
        dec_grad.transpose(0, 2, 1),
        error_sums[0].reshape(layers, d),
    )


def solution(mesh):
    finer = Mesh(
        mesh.devices.reshape(mesh.shape["grp"], mesh.shape["layer"], 2, 4, 2),
        (G, Z, X, Y, C),
    )
    return jax.shard_map(
        per_device,
        mesh=finer,
        in_specs=(
            P(Z, GRP_FEAT, None),
            P(GRP_FEAT, None, Z),
            P(Z, None, FEAT),
            P(Z, FEAT),
            P(None, FEAT, Z),
            P(None, Z),
        ),
        out_specs=(P(Z, G, FEAT), P(Z, FEAT), P(G, FEAT, Z), P(None, Z)),
        check_vma=False,
    )
```

```python
import jax
import jax.numpy as jnp
from jax import lax
from jax.experimental import pallas as pl
from jax.experimental.pallas import tpu as pltpu
from jax.sharding import Mesh
from jax.sharding import PartitionSpec as P

X, Y, C, Z, G = ("feat_0", "feat_1", "feat_2", "layer", "grp")
FEAT = (X, Y, C)
GRP_FEAT = (G, X, Y, C)
BF16, F32 = (jnp.bfloat16, jnp.float32)
VMEM = pl.BlockSpec(memory_space=pltpu.VMEM)
SMEM = pl.BlockSpec(memory_space=pltpu.SMEM)


def from_offset(x, axis, offset):
    size = lax.axis_size(axis)
    return lax.ppermute(x, axis, [((i + offset) % size, i) for i in range(size)])


def to_offset(x, axis, offset):
    return from_offset(x, axis, -offset)


def after(x, *earlier):
    return lax.optimization_barrier((x, *earlier))[0]


def size_of(shape, dtype):
    count = jnp.dtype(dtype).itemsize
    for n in shape:
        count *= n
    return count


def call(body, outs, place, args, scratch=(), flops=0, wait=()):
    outs = [*outs, ((8, 128), F32)]
    moved = sum(size_of(a.shape, a.dtype) for a in args) + sum(size_of(*o) for o in outs)
    held = moved + sum(size_of(*s) for s in scratch)
    first, last = 1 + len(args), 1 + len(args) + len(wait)

    def run(*refs):
        body(*refs[:first], *refs[last:])

    return pl.pallas_call(
        run,
        out_shape=[jax.ShapeDtypeStruct(s, d) for s, d in outs],
        in_specs=[SMEM] + [VMEM] * (len(args) + len(wait)),
        out_specs=[VMEM] * len(outs),
        scratch_shapes=[pltpu.VMEM(s, d) for s, d in scratch],
        cost_estimate=pl.CostEstimate(flops=flops, bytes_accessed=moved, transcendentals=0),
        compiler_params=pltpu.CompilerParams(vmem_limit_bytes=held + (4 << 20)),
    )(place, *args, *wait)


def lay_rows(parts, target):
    at = 0
    for part in parts:
        target[at : at + part.shape[0], :] = part[...]
        at += part.shape[0]


def encode(place, blocks, weight, bias):
    rows = sum(b.shape[0] for b in blocks)
    width, feats = weight.shape
    n = len(blocks)

    def body(_, *refs):
        parts, (w, b, joined, acts, mask, token) = refs[:n], refs[n:]
        token[...] = jnp.zeros_like(token)
        lay_rows(parts, joined)
        pre = jnp.dot(joined[...], w[...], preferred_element_type=F32) + b[...]
        acts[...] = jnp.maximum(pre, 0.0).astype(BF16)
        mask[...] = jnp.where(pre > 0, 1.0, 0.0).astype(BF16)

    return call(
        body,
        [((rows, width), BF16), ((rows, feats), BF16), ((rows, feats), BF16)],
        place,
        [*blocks, weight, bias],
        flops=2 * rows * width * feats,
    )


def fresh(x, edge):
    lane = lax.broadcasted_iota(jnp.int32, x.shape, 1)
    return jnp.where(lane >= edge, x, jnp.zeros_like(x))


def nt(a, b):
    return lax.dot_general(a, b, (((1,), (1,)), ((), ())), preferred_element_type=F32)


def nn(a, b):
    return jnp.dot(a, b, preferred_element_type=F32)


def decode(place, sources, weight, block, wait=()):
    rows, feats = sources[0].shape
    half = rows // 2
    d = block
    wide = 4 * d
    e = d % 128

    def body(at_ref, *refs):
        a0, a1, a3, a2, b2, w, acts, keep, send, token = refs
        token[...] = jnp.zeros_like(token)
        for step, part in ((0, a0), (1, a1), (3, a3)):
            acts[lax.rem(at_ref[0] + step, 4)] = part[...]
        layer = lax.rem(at_ref[0] + 2, 4)
        acts[layer, :half, :] = a2[...]
        acts[layer, half:, :] = b2[...]
        for at, out in ((half, send), (0, keep)):
            a = [acts[s, at : at + half, :] for s in range(4)]
            out[:, : d - e] = nt(a[0], w[: d - e, :]).astype(BF16)
            part = nt(a[0], w[d - e : 2 * d, :]) + fresh(nt(a[1], w[4 * d - e : 5 * d, :]), e)
            out[:, d - e : 2 * d] = part.astype(BF16)
            part = (
                nt(a[0], w[2 * d : 3 * d - e, :])
                + nt(a[1], w[5 * d : 6 * d - e, :])
                + nt(a[2], w[7 * d : 8 * d - e, :])
            )
            out[:, 2 * d : 3 * d - e] = part.astype(BF16)
            part = (
                nt(a[0], w[3 * d - e : 4 * d, :])
                + nt(a[1], w[6 * d - e : 7 * d, :])
                + nt(a[2], w[8 * d - e : 9 * d, :])
                + fresh(nt(a[3], w[9 * d - e :, :]), e)
            )
            out[:, 3 * d - e :] = part.astype(BF16)

    return call(
        body,
        [((4, rows, feats), BF16), ((half, wide), BF16), ((half, wide), BF16)],
        place,
        [*sources, weight],
        flops=20 * rows * feats * d,
        wait=wait,
    )


def feature_grads(place, blocks, weight, block):
    rows = sum(b.shape[0] for b in blocks)
    feats = weight.shape[1]
    d = block
    e = d % 128
    half = rows // 2
    n = len(blocks)

    def body(at_ref, *refs):
        parts, (w, own, up, down, a1, b3, token, held, joined) = refs[:n], refs[n:]
        token[...] = jnp.zeros_like(token)
        lay_rows(parts, joined)

        def slot(layer):
            return lax.rem(layer + 4 - at_ref[0], 4)

        x = joined[...]
        held[slot(0)] = nn(x, w[: 4 * d, :]).astype(BF16)
        part = jnp.concatenate([fresh(x[:, d - e : d - e + 128], e), x[:, d - e + 128 :]], axis=1)
        held[slot(1)] = nn(part, w[4 * d - e : 7 * d, :]).astype(BF16)
        held[slot(2)] = nn(x[:, 2 * d :], w[7 * d : 9 * d, :]).astype(BF16)
        part = jnp.concatenate([fresh(x[:, 3 * d - e : 3 * d - e + 128], e), x[:, 3 * d - e + 128 :]], axis=1)
        held[slot(3)] = nn(part, w[9 * d - e :, :]).astype(BF16)
        own[...] = held[0]
        up[:half, :] = held[2, :half, :]
        up[half:, :] = held[1, half:, :]
        down[:half, :] = held[3, :half, :]
        down[half:, :] = held[2, half:, :]
        a1[...] = held[1, :half, :]
        b3[...] = held[3, half:, :]

    return call(
        body,
        [((rows, feats), BF16)] * 3 + [((half, feats), BF16)] * 2,
        place,
        [*blocks, weight],
        scratch=[((4, rows, feats), BF16), ((rows, 4 * d), BF16)],
        flops=20 * rows * feats * d,
    )


NEAR = ((0, 0), (1, 0), (0, 1), (0, 3))
FAR = ((1, 1), (1, 3), (0, 2), (1, 2))
PAIRS = tuple((s, t) for s in range(4) for t in range(s, 4))


def own_pairs_grad(place, acts, errors, other_acts, other_errors, block):
    _, rows, feats = acts[0].shape
    d = block
    wide = 4 * d
    tokens = other_errors.shape[1]
    count = 4 * rows
    own = len(PAIRS) // 2

    def body(at_ref, a0, a1, x0, x1, x2, x3, a2, others, out, total, token, turned, laid):
        token[...] = jnp.zeros_like(token)
        at = 0
        for blocks in (NEAR, FAR):
            for core in range(2):
                for dx, dy in blocks:
                    x = lax.rem(at_ref[2] + dx, 2)
                    y = lax.rem(at_ref[3] + dy, 4)
                    c = lax.rem(at_ref[4] + core, 2)
                    laid[at : at + tokens, :] = others[(x * 4 + y) * 2 + c]
                    at += tokens
        sums = jnp.zeros((8, wide), F32)
        at = 0
        for part in (x0, x1, x2, x3, laid):
            x = part[...]
            size = x.shape[0]
            sums += nn(jnp.ones((8, size), BF16), x)
            for t in range(4):
                low = t * d // 128 * 128
                turned[t, :, at : at + size] = x[:, low : (t + 1) * d].T[t * d - low :]
            at += size
        total[...] = sums
        first = at_ref[1] == 0
        for i in range(own):
            s, t = [jnp.where(first, m, n) for m, n in zip(PAIRS[i], PAIRS[own + i])]
            part = nn(turned[t, :, :rows], a0[s]) + nn(turned[t, :, rows : 2 * rows], a1[s])
            out[i] = (part + nn(turned[t, :, 2 * rows :], a2[s])).astype(BF16)

    return call(
        body,
        [((own, d, feats), BF16), ((8, wide), F32)],
        place,
        [*acts, *errors, other_acts, other_errors],
        scratch=[((4, d, count), BF16), ((2 * rows, wide), BF16)],
        flops=10 * count * feats * d,
    )


def gather_rows(block, use, before_far=()):
    half = block.shape[0] // 2
    x1 = from_offset(block, X, 1)
    y1 = from_offset(block, Y, 1)
    y3 = from_offset(block, Y, -1)
    near = jnp.concatenate([block, x1, y1, y3], axis=0)
    xy1 = from_offset(y1, X, 1)
    xy3 = from_offset(x1, Y, -1)
    y2 = from_offset(y1, Y, 1)
    near_core = from_offset(near, C, 1)
    first, made = use([near, near_core], ())
    xy2a, xy2b = after((xy1[:half], xy3[half:]), made)
    xy2a = from_offset(xy2a, Y, 1)
    xy2b = from_offset(xy2b, Y, -1)
    far = jnp.concatenate([xy1, xy3, y2, xy2a, xy2b], axis=0)
    far_core = from_offset(far, C, 1)
    return first, use([far, far_core], before_far)[0]


def sum_rows(near, far):
    rows = near[0].shape[0] // 4
    half = rows // 2
    near_in = from_offset(near[1], C, 1)
    far_in = from_offset(far[1], C, 1)

    def taken(pair, arrived, k):
        cut = slice(k * rows, (k + 1) * rows)
        return pair[cut].astype(F32) + arrived[cut].astype(F32)

    q00, q10, q01, q03 = [taken(near[0], near_in, k) for k in range(4)]
    q11, q13, q02, q12 = [taken(far[0], far_in, k) for k in range(4)]
    r03 = to_offset(q03.astype(BF16), Y, -1)
    a = to_offset(q12[:half].astype(BF16), Y, 1).astype(F32)
    b = to_offset(q12[half:].astype(BF16), Y, -1).astype(F32)
    r02 = to_offset(q02.astype(BF16), Y, 1)
    q11 = jnp.concatenate([q11[:half] + a, q11[half:]], axis=0)
    q13 = jnp.concatenate([q13[:half], q13[half:] + b], axis=0)
    r11 = to_offset(q11.astype(BF16), X, 1)
    r13 = to_offset(q13.astype(BF16), Y, -1)
    q01 = q01 + r11.astype(F32) + r02.astype(F32)
    q10 = q10 + r13.astype(F32)
    r01 = to_offset(q01.astype(BF16), Y, 1)
    r10 = to_offset(q10.astype(BF16), X, 1)
    return q00, r03, r01, r10


def scaled_errors(place, parts, targets, bias, tokens):
    rows, layers, d = targets.shape

    def body(_, a, b, c, e, targets_ref, bias_ref, out, token):
        token[...] = jnp.zeros_like(token)
        total = a[...] + b[...].astype(F32) + c[...].astype(F32) + e[...].astype(F32)
        wanted = [targets_ref[:, t, :].astype(F32) - bias_ref[t : t + 1, :] for t in range(layers)]
        out[...] = ((total - jnp.concatenate(wanted, axis=1)) / tokens).astype(BF16)

    return call(body, [((rows, layers * d), BF16)], place, [*parts, targets, bias])[0]


def gather_layers(acts):
    half = acts.shape[0] // 2
    a1 = from_offset(acts, Z, 1)
    a3 = from_offset(acts, Z, -1)
    a2 = from_offset(a1[:half], Z, 1)
    b2 = from_offset(a3[half:], Z, -1)
    return acts, a1, a3, a2, b2


def sum_layers(own, up, down, a1, b3):
    half = a1.shape[0]
    up = to_offset(up, Z, 1)
    down = to_offset(down, Z, -1)
    gate = (up, down)
    a1 = to_offset((a1.astype(F32) + up[:half].astype(F32)).astype(BF16), Z, 1)
    b3 = to_offset((b3.astype(F32) + down[half:].astype(F32)).astype(BF16), Z, -1)
    first = own[:half].astype(F32) + a1.astype(F32) + down[:half].astype(F32)
    second = own[half:].astype(F32) + up[half:].astype(F32) + b3.astype(F32)
    return jnp.concatenate([first, second], axis=0), gate


def exchanged(x, meanwhile):
    own = lax.axis_index(G)
    half = x.shape[0] // 2
    sent = lax.dynamic_slice_in_dim(x, (1 - own) * half, half, 0)
    kept = lax.dynamic_slice_in_dim(x, own * half, half, 0)
    arrived = after(from_offset(sent, G, 1), meanwhile(sent))
    return (kept.astype(F32) + arrived.astype(F32)).astype(x.dtype)


def per_device(inputs, targets, enc_weight, enc_bias, dec_weight, dec_bias):
    layers, d = dec_bias.shape
    place = jnp.stack([lax.axis_index(axis) for axis in (Z, G, X, Y, C)]).astype(jnp.int32)
    tok_dev = inputs.shape[1]
    total_tokens = tok_dev * lax.axis_size(FEAT) * lax.axis_size(G)
    feats = dec_weight.shape[1]
    decoder = dec_weight.transpose(0, 2, 1).reshape(-1, feats)

    def forward(chunk, earlier):
        joined, acts, mask, _ = encode(after(place, *earlier), chunk, enc_weight[0], enc_bias)
        sources = gather_layers(acts)
        return (joined, mask, sources), acts

    near, far = gather_rows(inputs[0], forward)
    other_acts = from_offset(jnp.concatenate([near[2][0], far[2][0]], axis=0), G, 1)
    acts, keep, send, token = decode(place, near[2], decoder, d)
    acts, partial = [acts], [(keep, send)]
    far_acts, keep, send, _ = decode(after(place, other_acts), far[2], decoder, d, (token,))
    acts.append(far_acts)
    partial.append((keep, send))
    scaled = scaled_errors(place, sum_rows(*partial), targets, dec_bias, total_tokens)
    other_acts = lax.all_gather(other_acts, Z, axis=0)

    def backward(chunk, earlier):
        *parts, _ = feature_grads(after(place, *earlier), chunk, decoder, d)
        dacts, gate = sum_layers(*parts)
        return (chunk, dacts, gate, parts[0]), parts[0]

    other_errors = from_offset(scaled, G, 1)
    graded = gather_rows(scaled, backward, (other_acts,))
    other_errors = lax.all_gather(after(other_errors, *graded[0][2], graded[1][3], other_acts), FEAT, axis=0)
    dpre = [jnp.where(c[1] > 0, g[1], jnp.zeros_like(g[1])) for c, g in zip((near, far), graded)]
    enc_bias_grad = sum(jnp.sum(x, axis=0) for x in dpre)
    other_bias_grad = from_offset(enc_bias_grad, G, 1)
    enc_grad = sum(
        jnp.einsum("rd,rf->df", chunk[0], x.astype(BF16), preferred_element_type=F32)
        for chunk, x in zip((near, far), dpre)
    )
    made = []

    def meanwhile(sent):
        own_errors = [*graded[0][0], *graded[1][0]]
        made.extend(own_pairs_grad(after(place, sent), acts, own_errors, other_acts, other_errors, d))
        return made[1]

    enc_grad = exchanged(enc_grad.astype(BF16), meanwhile)
    dec_grad, error_sums, _ = made
    enc_bias_grad = enc_bias_grad + after(other_bias_grad, error_sums)
    return (
        enc_grad[None],
        enc_bias_grad[None],
        dec_grad.transpose(0, 2, 1),
        error_sums[0].reshape(layers, d),
    )


def solution(mesh):
    finer = Mesh(
        mesh.devices.reshape(mesh.shape["grp"], mesh.shape["layer"], 2, 4, 2),
        (G, Z, X, Y, C),
    )
    return jax.shard_map(
        per_device,
        mesh=finer,
        in_specs=(
            P(Z, GRP_FEAT, None),
            P(GRP_FEAT, None, Z),
            P(Z, None, FEAT),
            P(Z, FEAT),
            P(None, FEAT, Z),
            P(None, Z),
        ),
        out_specs=(P(Z, G, FEAT), P(Z, FEAT), P(G, FEAT, Z), P(None, Z)),
        check_vma=False,
    )
```

```python
import jax
import jax.numpy as jnp
from jax import lax
from jax.experimental import pallas as pl
from jax.experimental.pallas import tpu as pltpu
from jax.sharding import Mesh
from jax.sharding import PartitionSpec as P

X, Y, C, Z, G = ("feat_0", "feat_1", "feat_2", "layer", "grp")
FEAT = (X, Y, C)
GRP_FEAT = (G, X, Y, C)
BF16, F32 = (jnp.bfloat16, jnp.float32)
VMEM = pl.BlockSpec(memory_space=pltpu.VMEM)
SMEM = pl.BlockSpec(memory_space=pltpu.SMEM)


def from_offset(x, axis, offset):
    size = lax.axis_size(axis)
    return lax.ppermute(x, axis, [((i + offset) % size, i) for i in range(size)])


def to_offset(x, axis, offset):
    return from_offset(x, axis, -offset)


def after(x, *earlier):
    return lax.optimization_barrier((x, *earlier))[0]


def size_of(shape, dtype):
    count = jnp.dtype(dtype).itemsize
    for n in shape:
        count *= n
    return count


def call(body, outs, place, args, scratch=(), flops=0, wait=()):
    outs = [*outs, ((8, 128), F32)]
    moved = sum(size_of(a.shape, a.dtype) for a in args) + sum(size_of(*o) for o in outs)
    held = moved + sum(size_of(*s) for s in scratch)
    first, last = 1 + len(args), 1 + len(args) + len(wait)

    def run(*refs):
        body(*refs[:first], *refs[last:])

    return pl.pallas_call(
        run,
        out_shape=[jax.ShapeDtypeStruct(s, d) for s, d in outs],
        in_specs=[SMEM] + [VMEM] * (len(args) + len(wait)),
        out_specs=[VMEM] * len(outs),
        scratch_shapes=[pltpu.VMEM(s, d) for s, d in scratch],
        cost_estimate=pl.CostEstimate(flops=flops, bytes_accessed=moved, transcendentals=0),
        compiler_params=pltpu.CompilerParams(vmem_limit_bytes=held + (4 << 20)),
    )(place, *args, *wait)


def lay_rows(parts, target):
    at = 0
    for part in parts:
        target[at : at + part.shape[0], :] = part[...]
        at += part.shape[0]


def encode(place, blocks, weight, bias):
    rows = sum(b.shape[0] for b in blocks)
    width, feats = weight.shape
    n = len(blocks)

    def body(_, *refs):
        parts, (w, b, joined, acts, mask, token) = refs[:n], refs[n:]
        token[...] = jnp.zeros_like(token)
        lay_rows(parts, joined)
        pre = jnp.dot(joined[...], w[...], preferred_element_type=F32) + b[...]
        acts[...] = jnp.maximum(pre, 0.0).astype(BF16)
        mask[...] = jnp.where(pre > 0, 1.0, 0.0).astype(BF16)

    return call(
        body,
        [((rows, width), BF16), ((rows, feats), BF16), ((rows, feats), BF16)],
        place,
        [*blocks, weight, bias],
        flops=2 * rows * width * feats,
    )


def fresh(x, edge):
    lane = lax.broadcasted_iota(jnp.int32, x.shape, 1)
    return jnp.where(lane >= edge, x, jnp.zeros_like(x))


def nt(a, b):
    return lax.dot_general(a, b, (((1,), (1,)), ((), ())), preferred_element_type=F32)


def nn(a, b):
    return jnp.dot(a, b, preferred_element_type=F32)


def decode(place, sources, weight, block):
    rows, feats = sources[0].shape
    half = rows // 2
    d = block
    wide = 4 * d
    e = d % 128

    def body(at_ref, *refs):
        a0, a1, a3, a2, b2, w, acts, keep, send, token = refs
        token[...] = jnp.zeros_like(token)
        for step, part in ((0, a0), (1, a1), (3, a3)):
            acts[lax.rem(at_ref[0] + step, 4)] = part[...]
        layer = lax.rem(at_ref[0] + 2, 4)
        acts[layer, :half, :] = a2[...]
        acts[layer, half:, :] = b2[...]
        for at, out in ((half, send), (0, keep)):
            a = [acts[s, at : at + half, :] for s in range(4)]
            out[:, : d - e] = nt(a[0], w[: d - e, :]).astype(BF16)
            part = nt(a[0], w[d - e : 2 * d, :]) + fresh(nt(a[1], w[4 * d - e : 5 * d, :]), e)
            out[:, d - e : 2 * d] = part.astype(BF16)
            part = (
                nt(a[0], w[2 * d : 3 * d - e, :])
                + nt(a[1], w[5 * d : 6 * d - e, :])
                + nt(a[2], w[7 * d : 8 * d - e, :])
            )
            out[:, 2 * d : 3 * d - e] = part.astype(BF16)
            part = (
                nt(a[0], w[3 * d - e : 4 * d, :])
                + nt(a[1], w[6 * d - e : 7 * d, :])
                + nt(a[2], w[8 * d - e : 9 * d, :])
                + fresh(nt(a[3], w[9 * d - e :, :]), e)
            )
            out[:, 3 * d - e :] = part.astype(BF16)

    return call(
        body,
        [((4, rows, feats), BF16), ((half, wide), BF16), ((half, wide), BF16)],
        place,
        [*sources, weight],
        flops=20 * rows * feats * d,
    )


def feature_grads(place, blocks, weight, block):
    rows = sum(b.shape[0] for b in blocks)
    feats = weight.shape[1]
    d = block
    e = d % 128
    half = rows // 2
    n = len(blocks)

    def body(at_ref, *refs):
        parts, (w, own, up, down, a1, b3, token, held, joined) = refs[:n], refs[n:]
        token[...] = jnp.zeros_like(token)
        lay_rows(parts, joined)

        def slot(layer):
            return lax.rem(layer + 4 - at_ref[0], 4)

        x = joined[...]
        held[slot(0)] = nn(x, w[: 4 * d, :]).astype(BF16)
        part = jnp.concatenate([fresh(x[:, d - e : d - e + 128], e), x[:, d - e + 128 :]], axis=1)
        held[slot(1)] = nn(part, w[4 * d - e : 7 * d, :]).astype(BF16)
        held[slot(2)] = nn(x[:, 2 * d :], w[7 * d : 9 * d, :]).astype(BF16)
        part = jnp.concatenate([fresh(x[:, 3 * d - e : 3 * d - e + 128], e), x[:, 3 * d - e + 128 :]], axis=1)
        held[slot(3)] = nn(part, w[9 * d - e :, :]).astype(BF16)
        own[...] = held[0]
        up[:half, :] = held[2, :half, :]
        up[half:, :] = held[1, half:, :]
        down[:half, :] = held[3, :half, :]
        down[half:, :] = held[2, half:, :]
        a1[...] = held[1, :half, :]
        b3[...] = held[3, half:, :]

    return call(
        body,
        [((rows, feats), BF16)] * 3 + [((half, feats), BF16)] * 2,
        place,
        [*blocks, weight],
        scratch=[((4, rows, feats), BF16), ((rows, 4 * d), BF16)],
        flops=20 * rows * feats * d,
    )


NEAR = ((0, 0), (1, 0), (0, 1), (0, 3))
FAR = ((1, 1), (1, 3), (0, 2), (1, 2))
PAIRS = tuple((s, t) for s in range(4) for t in range(s, 4))


def own_pairs_grad(place, acts, errors, other_acts, other_errors, block):
    _, rows, feats = acts[0].shape
    d = block
    wide = 4 * d
    tokens = other_errors.shape[1]
    count = 4 * rows
    own = len(PAIRS) // 2

    def body(at_ref, a0, a1, *refs):
        parts, (a2, others, out, total, token, turned, laid) = refs[: len(errors)], refs[len(errors) :]
        token[...] = jnp.zeros_like(token)
        at = 0
        for blocks in (NEAR, FAR):
            for core in range(2):
                for dx, dy in blocks:
                    x = lax.rem(at_ref[2] + dx, 2)
                    y = lax.rem(at_ref[3] + dy, 4)
                    c = lax.rem(at_ref[4] + core, 2)
                    laid[at : at + tokens, :] = others[(x * 4 + y) * 2 + c]
                    at += tokens
        sums = jnp.zeros((8, wide), F32)
        at = 0
        near, near_core, far, last, far_core, last_core = [part[...] for part in parts]
        far = jnp.concatenate([far, last], axis=0)
        far_core = jnp.concatenate([far_core, last_core], axis=0)
        for x in (near, near_core, far, far_core, laid[...]):
            size = x.shape[0]
            sums += nn(jnp.ones((8, size), BF16), x)
            for t in range(4):
                low = t * d // 128 * 128
                turned[t, :, at : at + size] = x[:, low : (t + 1) * d].T[t * d - low :]
            at += size
        total[...] = sums
        first = at_ref[1] == 0
        for i in range(own):
            s, t = [jnp.where(first, m, n) for m, n in zip(PAIRS[i], PAIRS[own + i])]
            part = nn(turned[t, :, :rows], a0[s]) + nn(turned[t, :, rows : 2 * rows], a1[s])
            out[i] = (part + nn(turned[t, :, 2 * rows :], a2[s])).astype(BF16)

    return call(
        body,
        [((own, d, feats), BF16), ((8, wide), F32)],
        place,
        [*acts, *errors, other_acts, other_errors],
        scratch=[((4, d, count), BF16), ((2 * rows, wide), BF16)],
        flops=10 * count * feats * d,
    )


def gather_rows(block, use):
    half = block.shape[0] // 2
    x1 = from_offset(block, X, 1)
    y1 = from_offset(block, Y, 1)
    y3 = from_offset(block, Y, -1)
    near = jnp.concatenate([block, x1, y1, y3], axis=0)
    near_core = from_offset(near, C, 1)
    xy1 = from_offset(y1, X, 1)
    xy3 = from_offset(x1, Y, -1)
    y2 = from_offset(y1, Y, 1)
    xy2a = from_offset(xy1[:half], Y, 1)
    xy2b = from_offset(xy3[half:], Y, -1)
    first, made = use([near, near_core])
    far = jnp.concatenate([xy1, xy3, y2], axis=0)
    far_core = from_offset(far, C, 1)
    last = jnp.concatenate(after([xy2a, xy2b], made), axis=0)
    last_core = from_offset(last, C, 1)
    return first, use([far, last, far_core, last_core])[0]


def sum_rows(near_after, far):
    rows = far[0].shape[0] // 4
    half = rows // 2

    def taken(pair, arrived, k):
        cut = slice(k * rows, (k + 1) * rows)
        return pair[cut].astype(F32) + arrived[cut].astype(F32)

    far_in = from_offset(far[1], C, 1)
    q11, q13, q02, q12 = [taken(far[0], far_in, k) for k in range(4)]
    a = to_offset(q12[:half].astype(BF16), Y, 1)
    b = to_offset(q12[half:].astype(BF16), Y, -1)
    near = near_after(a, b)
    near_in = from_offset(near[1], C, 1)
    q00, q10, q01, q03 = [taken(near[0], near_in, k) for k in range(4)]
    r02 = to_offset(q02.astype(BF16), Y, 1)
    r03 = to_offset(q03.astype(BF16), Y, -1)
    q11 = jnp.concatenate([q11[:half] + a.astype(F32), q11[half:]], axis=0)
    q13 = jnp.concatenate([q13[:half], q13[half:] + b.astype(F32)], axis=0)
    r11 = to_offset(q11.astype(BF16), X, 1)
    r13 = to_offset(q13.astype(BF16), Y, -1)
    q01 = q01 + r11.astype(F32) + r02.astype(F32)
    q10 = q10 + r13.astype(F32)
    r01 = to_offset(q01.astype(BF16), Y, 1)
    r10 = to_offset(q10.astype(BF16), X, 1)
    return q00, r03, r01, r10


def scaled_errors(place, parts, targets, bias, tokens):
    rows, layers, d = targets.shape

    def body(_, a, b, c, e, targets_ref, bias_ref, out, token):
        token[...] = jnp.zeros_like(token)
        total = a[...] + b[...].astype(F32) + c[...].astype(F32) + e[...].astype(F32)
        wanted = [targets_ref[:, t, :].astype(F32) - bias_ref[t : t + 1, :] for t in range(layers)]
        out[...] = ((total - jnp.concatenate(wanted, axis=1)) / tokens).astype(BF16)

    return call(body, [((rows, layers * d), BF16)], place, [*parts, targets, bias])[0]


def gather_layers(acts):
    half = acts.shape[0] // 2
    a1 = from_offset(acts, Z, 1)
    a3 = from_offset(acts, Z, -1)
    a2 = from_offset(a1[:half], Z, 1)
    b2 = from_offset(a3[half:], Z, -1)
    return acts, a1, a3, a2, b2


def sum_layers(own, up, down, a1, b3):
    half = a1.shape[0]
    up = to_offset(up, Z, 1)
    down = to_offset(down, Z, -1)
    gate = (up, down)
    a1 = to_offset((a1.astype(F32) + up[:half].astype(F32)).astype(BF16), Z, 1)
    b3 = to_offset((b3.astype(F32) + down[half:].astype(F32)).astype(BF16), Z, -1)
    first = own[:half].astype(F32) + a1.astype(F32) + down[:half].astype(F32)
    second = own[half:].astype(F32) + up[half:].astype(F32) + b3.astype(F32)
    return jnp.concatenate([first, second], axis=0), gate


def exchanged(x, meanwhile):
    own = lax.axis_index(G)
    half = x.shape[0] // 2
    sent = lax.dynamic_slice_in_dim(x, (1 - own) * half, half, 0)
    kept = lax.dynamic_slice_in_dim(x, own * half, half, 0)
    arrived = after(from_offset(sent, G, 1), meanwhile(sent))
    return (kept.astype(F32) + arrived.astype(F32)).astype(x.dtype)


def per_device(inputs, targets, enc_weight, enc_bias, dec_weight, dec_bias):
    layers, d = dec_bias.shape
    place = jnp.stack([lax.axis_index(axis) for axis in (Z, G, X, Y, C)]).astype(jnp.int32)
    tok_dev = inputs.shape[1]
    total_tokens = tok_dev * lax.axis_size(FEAT) * lax.axis_size(G)
    feats = dec_weight.shape[1]
    decoder = dec_weight.transpose(0, 2, 1).reshape(-1, feats)

    def forward(chunk):
        joined, acts, mask, _ = encode(place, chunk, enc_weight[0], enc_bias)
        sources = gather_layers(acts)
        return (joined, mask, sources), acts

    near, far = gather_rows(inputs[0], forward)
    other_acts = [from_offset(chunk[2][0], G, 1) for chunk in (near, far)]
    far_acts, *far_rows, _ = decode(after(place, *other_acts, *near[2][3:]), far[2], decoder, d)
    acts = []

    def near_after(*earlier):
        near_acts, *near_rows, _ = decode(after(place, *earlier), near[2], decoder, d)
        acts.extend([near_acts, far_acts])
        return near_rows

    parts = sum_rows(near_after, far_rows)
    scaled = scaled_errors(place, parts, targets, dec_bias, total_tokens)
    other_acts = lax.all_gather(jnp.concatenate(other_acts, axis=0), Z, axis=0)

    def backward(chunk):
        *parts, _ = feature_grads(place, chunk, decoder, d)
        dacts, gate = sum_layers(*parts)
        return (chunk, dacts, gate, parts[0]), parts[0]

    other_errors = from_offset(scaled, G, 1)
    graded = gather_rows(scaled, backward)
    other_errors = lax.all_gather(after(other_errors, *graded[0][2], graded[1][3], other_acts), FEAT, axis=0)
    dpre = [jnp.where(c[1] > 0, g[1], jnp.zeros_like(g[1])) for c, g in zip((near, far), graded)]
    enc_bias_grad = sum(jnp.sum(x, axis=0) for x in dpre)
    other_bias_grad = from_offset(enc_bias_grad, G, 1)
    enc_grad = sum(
        jnp.einsum("rd,rf->df", chunk[0], x.astype(BF16), preferred_element_type=F32)
        for chunk, x in zip((near, far), dpre)
    )
    made = []

    def meanwhile(sent):
        own_errors = [*graded[0][0], *graded[1][0]]
        made.extend(own_pairs_grad(after(place, sent), acts, own_errors, other_acts, other_errors, d))
        return made[1]

    enc_grad = exchanged(enc_grad.astype(BF16), meanwhile)
    dec_grad, error_sums, _ = made
    enc_bias_grad = enc_bias_grad + after(other_bias_grad, error_sums)
    return (
        enc_grad[None],
        enc_bias_grad[None],
        dec_grad.transpose(0, 2, 1),
        error_sums[0].reshape(layers, d),
    )


def solution(mesh):
    finer = Mesh(
        mesh.devices.reshape(mesh.shape["grp"], mesh.shape["layer"], 2, 4, 2),
        (G, Z, X, Y, C),
    )
    return jax.shard_map(
        per_device,
        mesh=finer,
        in_specs=(
            P(Z, GRP_FEAT, None),
            P(GRP_FEAT, None, Z),
            P(Z, None, FEAT),
            P(Z, FEAT),
            P(None, FEAT, Z),
            P(None, Z),
        ),
        out_specs=(P(Z, G, FEAT), P(Z, FEAT), P(G, FEAT, Z), P(None, Z)),
        check_vma=False,
    )
```

```python
import jax
import jax.numpy as jnp
from jax import lax
from jax.experimental import pallas as pl
from jax.experimental.pallas import tpu as pltpu
from jax.sharding import Mesh
from jax.sharding import PartitionSpec as P

X, Y, C, Z, G = ("feat_0", "feat_1", "feat_2", "layer", "grp")
FEAT = (X, Y, C)
GRP_FEAT = (G, X, Y, C)
BF16, F32 = (jnp.bfloat16, jnp.float32)
VMEM = pl.BlockSpec(memory_space=pltpu.VMEM)
SMEM = pl.BlockSpec(memory_space=pltpu.SMEM)


def from_offset(x, axis, offset):
    size = lax.axis_size(axis)
    return lax.ppermute(x, axis, [((i + offset) % size, i) for i in range(size)])


def to_offset(x, axis, offset):
    return from_offset(x, axis, -offset)


def after(x, *earlier):
    return lax.optimization_barrier((x, *earlier))[0]


def size_of(shape, dtype):
    count = jnp.dtype(dtype).itemsize
    for n in shape:
        count *= n
    return count


def call(body, outs, place, args, scratch=(), flops=0, wait=()):
    outs = [*outs, ((8, 128), F32)]
    moved = sum(size_of(a.shape, a.dtype) for a in args) + sum(size_of(*o) for o in outs)
    held = moved + sum(size_of(*s) for s in scratch)
    first, last = 1 + len(args), 1 + len(args) + len(wait)

    def run(*refs):
        body(*refs[:first], *refs[last:])

    return pl.pallas_call(
        run,
        out_shape=[jax.ShapeDtypeStruct(s, d) for s, d in outs],
        in_specs=[SMEM] + [VMEM] * (len(args) + len(wait)),
        out_specs=[VMEM] * len(outs),
        scratch_shapes=[pltpu.VMEM(s, d) for s, d in scratch],
        cost_estimate=pl.CostEstimate(flops=flops, bytes_accessed=moved, transcendentals=0),
        compiler_params=pltpu.CompilerParams(vmem_limit_bytes=held + (4 << 20)),
    )(place, *args, *wait)


def lay_rows(parts, target):
    at = 0
    for part in parts:
        target[at : at + part.shape[0], :] = part[...]
        at += part.shape[0]


def encode(place, blocks, weight, bias):
    rows = sum(b.shape[0] for b in blocks)
    width, feats = weight.shape
    n = len(blocks)

    def body(_, *refs):
        parts, (w, b, joined, acts, mask, token) = refs[:n], refs[n:]
        token[...] = jnp.zeros_like(token)
        lay_rows(parts, joined)
        pre = jnp.dot(joined[...], w[...], preferred_element_type=F32) + b[...]
        acts[...] = jnp.maximum(pre, 0.0).astype(BF16)
        mask[...] = jnp.where(pre > 0, 1.0, 0.0).astype(BF16)

    return call(
        body,
        [((rows, width), BF16), ((rows, feats), BF16), ((rows, feats), BF16)],
        place,
        [*blocks, weight, bias],
        flops=2 * rows * width * feats,
    )


def fresh(x, edge):
    lane = lax.broadcasted_iota(jnp.int32, x.shape, 1)
    return jnp.where(lane >= edge, x, jnp.zeros_like(x))


def nt(a, b):
    return lax.dot_general(a, b, (((1,), (1,)), ((), ())), preferred_element_type=F32)


def nn(a, b):
    return jnp.dot(a, b, preferred_element_type=F32)


def decode(place, sources, weight, block):
    rows, feats = sources[0].shape
    half = rows // 2
    d = block
    wide = 4 * d
    e = d % 128

    def body(at_ref, *refs):
        a0, a1, a3, a2, b2, w, acts, keep, send, token = refs
        token[...] = jnp.zeros_like(token)
        for step, part in ((0, a0), (1, a1), (3, a3)):
            acts[lax.rem(at_ref[0] + step, 4)] = part[...]
        layer = lax.rem(at_ref[0] + 2, 4)
        acts[layer, :half, :] = a2[...]
        acts[layer, half:, :] = b2[...]
        for at, out in ((half, send), (0, keep)):
            a = [acts[s, at : at + half, :] for s in range(4)]
            out[:, : d - e] = nt(a[0], w[: d - e, :]).astype(BF16)
            part = nt(a[0], w[d - e : 2 * d, :]) + fresh(nt(a[1], w[4 * d - e : 5 * d, :]), e)
            out[:, d - e : 2 * d] = part.astype(BF16)
            part = (
                nt(a[0], w[2 * d : 3 * d - e, :])
                + nt(a[1], w[5 * d : 6 * d - e, :])
                + nt(a[2], w[7 * d : 8 * d - e, :])
            )
            out[:, 2 * d : 3 * d - e] = part.astype(BF16)
            part = (
                nt(a[0], w[3 * d - e : 4 * d, :])
                + nt(a[1], w[6 * d - e : 7 * d, :])
                + nt(a[2], w[8 * d - e : 9 * d, :])
                + fresh(nt(a[3], w[9 * d - e :, :]), e)
            )
            out[:, 3 * d - e :] = part.astype(BF16)

    return call(
        body,
        [((4, rows, feats), BF16), ((half, wide), BF16), ((half, wide), BF16)],
        place,
        [*sources, weight],
        flops=20 * rows * feats * d,
    )


def feature_grads(place, blocks, weight, block):
    rows = sum(b.shape[0] for b in blocks)
    feats = weight.shape[1]
    d = block
    e = d % 128
    half = rows // 2
    n = len(blocks)

    def body(at_ref, *refs):
        parts, (w, own, up, down, a1, b3, token, held, joined) = refs[:n], refs[n:]
        token[...] = jnp.zeros_like(token)
        lay_rows(parts, joined)

        def slot(layer):
            return lax.rem(layer + 4 - at_ref[0], 4)

        x = joined[...]
        held[slot(0)] = nn(x, w[: 4 * d, :]).astype(BF16)
        part = jnp.concatenate([fresh(x[:, d - e : d - e + 128], e), x[:, d - e + 128 :]], axis=1)
        held[slot(1)] = nn(part, w[4 * d - e : 7 * d, :]).astype(BF16)
        held[slot(2)] = nn(x[:, 2 * d :], w[7 * d : 9 * d, :]).astype(BF16)
        part = jnp.concatenate([fresh(x[:, 3 * d - e : 3 * d - e + 128], e), x[:, 3 * d - e + 128 :]], axis=1)
        held[slot(3)] = nn(part, w[9 * d - e :, :]).astype(BF16)
        own[...] = held[0]
        up[:half, :] = held[2, :half, :]
        up[half:, :] = held[1, half:, :]
        down[:half, :] = held[3, :half, :]
        down[half:, :] = held[2, half:, :]
        a1[...] = held[1, :half, :]
        b3[...] = held[3, half:, :]

    return call(
        body,
        [((rows, feats), BF16)] * 3 + [((half, feats), BF16)] * 2,
        place,
        [*blocks, weight],
        scratch=[((4, rows, feats), BF16), ((rows, 4 * d), BF16)],
        flops=20 * rows * feats * d,
    )


NEAR = ((0, 0), (1, 0), (0, 1), (0, 3))
FAR = ((1, 1), (1, 3), (0, 2), (1, 2))
PAIRS = tuple((s, t) for s in range(4) for t in range(s, 4))


def lay_in_order(at_ref, blocks, target):
    tokens = blocks.shape[1]
    at = 0
    for chunk in (NEAR, FAR):
        for core in range(2):
            for dx, dy in chunk:
                x = lax.rem(at_ref[2] + dx, 2)
                y = lax.rem(at_ref[3] + dy, 4)
                c = lax.rem(at_ref[4] + core, 2)
                target[at : at + tokens, :] = blocks[(x * 4 + y) * 2 + c]
                at += tokens


def encoder_grad(place, rows, grads):
    half, feats = rows[0].shape[1] // 2, grads[0].shape[1]

    def body(at_ref, r0, r1, g0, g1, out, token):
        token[...] = jnp.zeros_like(token)
        own = pl.ds(pl.multiple_of(at_ref[1] * half, 128), half)
        out[...] = nn(r0[:, own].T, g0[...]) + nn(r1[:, own].T, g1[...])

    flops = 4 * rows[0].shape[0] * half * feats
    return call(body, [((half, feats), F32)], place, [*rows, *grads], flops=flops)[0]


def encoder_grad_sum(place, total, blocks, grads):
    count, tokens, half = blocks.shape
    rows, feats = grads[0].shape

    def body(at_ref, sum_ref, blocks_ref, g0, g1, out, token, laid):
        token[...] = jnp.zeros_like(token)
        lay_in_order(at_ref, blocks_ref, laid)
        part = nn(laid[:rows, :].T, g0[...]) + nn(laid[rows:, :].T, g1[...])
        out[...] = (sum_ref[...] + part).astype(BF16)

    return call(
        body,
        [((half, feats), BF16)],
        place,
        [total, blocks, *grads],
        scratch=[((count * tokens, half), BF16)],
        flops=4 * rows * half * feats,
    )[0]


def own_pairs_grad(place, acts, errors, other_acts, other_errors, block):
    _, rows, feats = acts[0].shape
    d = block
    wide = 4 * d
    count = 4 * rows
    own = len(PAIRS) // 2

    def body(at_ref, a0, a1, *refs):
        parts, (a2, others, out, total, token, turned, laid) = refs[: len(errors)], refs[len(errors) :]
        token[...] = jnp.zeros_like(token)
        lay_in_order(at_ref, others, laid)
        sums = jnp.zeros((8, wide), F32)
        at = 0
        near, near_core, far, last, far_core, last_core = [part[...] for part in parts]
        far = jnp.concatenate([far, last], axis=0)
        far_core = jnp.concatenate([far_core, last_core], axis=0)
        for x in (near, near_core, far, far_core, laid[...]):
            size = x.shape[0]
            sums += nn(jnp.ones((8, size), BF16), x)
            for t in range(4):
                low = t * d // 128 * 128
                turned[t, :, at : at + size] = x[:, low : (t + 1) * d].T[t * d - low :]
            at += size
        total[...] = sums
        first = at_ref[1] == 0
        for i in range(own):
            s, t = [jnp.where(first, m, n) for m, n in zip(PAIRS[i], PAIRS[own + i])]
            part = nn(turned[t, :, :rows], a0[s]) + nn(turned[t, :, rows : 2 * rows], a1[s])
            out[i] = (part + nn(turned[t, :, 2 * rows :], a2[s])).astype(BF16)

    return call(
        body,
        [((own, d, feats), BF16), ((8, wide), F32)],
        place,
        [*acts, *errors, other_acts, other_errors],
        scratch=[((4, d, count), BF16), ((2 * rows, wide), BF16)],
        flops=10 * count * feats * d,
    )


def gather_rows(block, use):
    half = block.shape[0] // 2
    x1 = from_offset(block, X, 1)
    y1 = from_offset(block, Y, 1)
    y3 = from_offset(block, Y, -1)
    near = jnp.concatenate([block, x1, y1, y3], axis=0)
    near_core = from_offset(near, C, 1)
    xy1 = from_offset(y1, X, 1)
    xy3 = from_offset(x1, Y, -1)
    y2 = from_offset(y1, Y, 1)
    xy2a = from_offset(xy1[:half], Y, 1)
    xy2b = from_offset(xy3[half:], Y, -1)
    first, made = use([near, near_core])
    far = jnp.concatenate([xy1, xy3, y2], axis=0)
    far_core = from_offset(far, C, 1)
    last = jnp.concatenate(after([xy2a, xy2b], made), axis=0)
    last_core = from_offset(last, C, 1)
    return first, use([far, last, far_core, last_core])[0]


def sum_rows(near_after, far):
    rows = far[0].shape[0] // 4
    half = rows // 2

    def taken(pair, arrived, k):
        cut = slice(k * rows, (k + 1) * rows)
        return pair[cut].astype(F32) + arrived[cut].astype(F32)

    far_in = from_offset(far[1], C, 1)
    q11, q13, q02, q12 = [taken(far[0], far_in, k) for k in range(4)]
    a = to_offset(q12[:half].astype(BF16), Y, 1)
    b = to_offset(q12[half:].astype(BF16), Y, -1)
    near = near_after(a, b)
    near_in = from_offset(near[1], C, 1)
    q00, q10, q01, q03 = [taken(near[0], near_in, k) for k in range(4)]
    r02 = to_offset(q02.astype(BF16), Y, 1)
    r03 = to_offset(q03.astype(BF16), Y, -1)
    q11 = jnp.concatenate([q11[:half] + a.astype(F32), q11[half:]], axis=0)
    q13 = jnp.concatenate([q13[:half], q13[half:] + b.astype(F32)], axis=0)
    r11 = to_offset(q11.astype(BF16), X, 1)
    r13 = to_offset(q13.astype(BF16), Y, -1)
    q01 = q01 + r11.astype(F32) + r02.astype(F32)
    q10 = q10 + r13.astype(F32)
    r01 = to_offset(q01.astype(BF16), Y, 1)
    r10 = to_offset(q10.astype(BF16), X, 1)
    return q00, r03, r01, r10


def scaled_errors(place, parts, targets, bias, tokens):
    rows, layers, d = targets.shape

    def body(_, a, b, c, e, targets_ref, bias_ref, out, token):
        token[...] = jnp.zeros_like(token)
        total = a[...] + b[...].astype(F32) + c[...].astype(F32) + e[...].astype(F32)
        wanted = [targets_ref[:, t, :].astype(F32) - bias_ref[t : t + 1, :] for t in range(layers)]
        out[...] = ((total - jnp.concatenate(wanted, axis=1)) / tokens).astype(BF16)

    return call(body, [((rows, layers * d), BF16)], place, [*parts, targets, bias])[0]


def gather_layers(acts):
    half = acts.shape[0] // 2
    a1 = from_offset(acts, Z, 1)
    a3 = from_offset(acts, Z, -1)
    a2 = from_offset(a1[:half], Z, 1)
    b2 = from_offset(a3[half:], Z, -1)
    return acts, a1, a3, a2, b2


def sum_layers(own, up, down, a1, b3):
    half = a1.shape[0]
    a1 = to_offset((a1.astype(F32) + up[:half].astype(F32)).astype(BF16), Z, 1)
    b3 = to_offset((b3.astype(F32) + down[half:].astype(F32)).astype(BF16), Z, -1)
    first = own[:half].astype(F32) + a1.astype(F32) + down[:half].astype(F32)
    second = own[half:].astype(F32) + up[half:].astype(F32) + b3.astype(F32)
    return jnp.concatenate([first, second], axis=0)


def per_device(inputs, targets, enc_weight, enc_bias, dec_weight, dec_bias):
    layers, d = dec_bias.shape
    place = jnp.stack([lax.axis_index(axis) for axis in (Z, G, X, Y, C)]).astype(jnp.int32)
    tok_dev = inputs.shape[1]
    total_tokens = tok_dev * lax.axis_size(FEAT) * lax.axis_size(G)
    feats = dec_weight.shape[1]
    decoder = dec_weight.transpose(0, 2, 1).reshape(-1, feats)

    def forward(chunk):
        joined, acts, mask, _ = encode(place, chunk, enc_weight[0], enc_bias)
        sources = gather_layers(acts)
        return (joined, mask, sources), acts

    near, far = gather_rows(inputs[0], forward)
    other_acts = [from_offset(chunk[2][0], G, 1) for chunk in (near, far)]
    far_acts, *far_rows, _ = decode(after(place, *other_acts, *near[2][3:]), far[2], decoder, d)
    acts = []

    def near_after(*earlier):
        near_acts, *near_rows, _ = decode(after(place, *earlier), near[2], decoder, d)
        acts.extend([near_acts, far_acts])
        return near_rows

    parts = sum_rows(near_after, far_rows)
    scaled = scaled_errors(place, parts, targets, dec_bias, total_tokens)
    group = lax.axis_index(G)
    half = inputs.shape[2] // 2
    other_rows = from_offset(lax.dynamic_slice_in_dim(inputs[0], (1 - group) * half, half, 1), G, 1)
    other_rows = lax.all_gather(after(other_rows, far[2][0]), FEAT, axis=0)
    other_acts = lax.all_gather(after(jnp.concatenate(other_acts, axis=0), other_rows), Z, axis=0)

    def backward(chunk):
        own, up, down, a1, b3, _ = feature_grads(place, chunk, decoder, d)
        return (chunk, (own, to_offset(up, Z, 1), to_offset(down, Z, -1)), (a1, b3)), own

    other_errors = from_offset(scaled, G, 1)
    graded = gather_rows(scaled, backward)
    (near_errors, near_hop, near_rest), (far_errors, far_hop, far_rest) = graded
    near_rest = after(near_rest, far_hop[0])
    dacts = [sum_layers(*near_hop, *near_rest), sum_layers(*far_hop, *far_rest)]
    other_errors = lax.all_gather(after(other_errors, *far_errors[2:], other_acts), FEAT, axis=0)
    dpre = [jnp.where(c[1] > 0, x, jnp.zeros_like(x)) for c, x in zip((near, far), dacts)]
    enc_bias_grad = sum(jnp.sum(x, axis=0) for x in dpre)
    dpre = [x.astype(BF16) for x in dpre]
    other_dpre = [from_offset(x, G, 1) for x in dpre]
    other_bias_grad = from_offset(enc_bias_grad, G, 1)
    enc_grad = encoder_grad(place, [near[0], far[0]], dpre)
    own_errors = [*near_errors, *far_errors]
    dec_grad, error_sums, _ = own_pairs_grad(after(place, enc_grad), acts, own_errors, other_acts, other_errors, d)
    enc_grad = encoder_grad_sum(after(place, error_sums), enc_grad, other_rows, other_dpre)
    enc_bias_grad = enc_bias_grad + after(other_bias_grad, error_sums)
    return (
        enc_grad[None],
        enc_bias_grad[None],
        dec_grad.transpose(0, 2, 1),
        error_sums[0].reshape(layers, d),
    )


def solution(mesh):
    finer = Mesh(
        mesh.devices.reshape(mesh.shape["grp"], mesh.shape["layer"], 2, 4, 2),
        (G, Z, X, Y, C),
    )
    return jax.shard_map(
        per_device,
        mesh=finer,
        in_specs=(
            P(Z, GRP_FEAT, None),
            P(GRP_FEAT, None, Z),
            P(Z, None, FEAT),
            P(Z, FEAT),
            P(None, FEAT, Z),
            P(None, Z),
        ),
        out_specs=(P(Z, G, FEAT), P(Z, FEAT), P(G, FEAT, Z), P(None, Z)),
        check_vma=False,
    )
```

```python
import jax
import jax.numpy as jnp
from jax import lax
from jax.experimental import pallas as pl
from jax.experimental.pallas import tpu as pltpu
from jax.sharding import Mesh
from jax.sharding import PartitionSpec as P

X, Y, C, Z, G = ("feat_0", "feat_1", "feat_2", "layer", "grp")
FEAT = (X, Y, C)
GRP_FEAT = (G, X, Y, C)
BF16, F32 = (jnp.bfloat16, jnp.float32)
VMEM = pl.BlockSpec(memory_space=pltpu.VMEM)
SMEM = pl.BlockSpec(memory_space=pltpu.SMEM)


def from_offset(x, axis, offset):
    size = lax.axis_size(axis)
    return lax.ppermute(x, axis, [((i + offset) % size, i) for i in range(size)])


def to_offset(x, axis, offset):
    return from_offset(x, axis, -offset)


def after(x, *earlier):
    return lax.optimization_barrier((x, *earlier))[0]


def size_of(shape, dtype):
    count = jnp.dtype(dtype).itemsize
    for n in shape:
        count *= n
    return count


def call(body, outs, place, args, scratch=(), flops=0, wait=()):
    outs = [*outs, ((8, 128), F32)]
    moved = sum(size_of(a.shape, a.dtype) for a in args) + sum(size_of(*o) for o in outs)
    held = moved + sum(size_of(*s) for s in scratch)
    first, last = 1 + len(args), 1 + len(args) + len(wait)

    def run(*refs):
        body(*refs[:first], *refs[last:])

    return pl.pallas_call(
        run,
        out_shape=[jax.ShapeDtypeStruct(s, d) for s, d in outs],
        in_specs=[SMEM] + [VMEM] * (len(args) + len(wait)),
        out_specs=[VMEM] * len(outs),
        scratch_shapes=[pltpu.VMEM(s, d) for s, d in scratch],
        cost_estimate=pl.CostEstimate(flops=flops, bytes_accessed=moved, transcendentals=0),
        compiler_params=pltpu.CompilerParams(vmem_limit_bytes=held + (4 << 20)),
    )(place, *args, *wait)


def lay_rows(parts, target):
    at = 0
    for part in parts:
        target[at : at + part.shape[0], :] = part[...]
        at += part.shape[0]


def encode(place, blocks, weight, bias):
    rows = sum(b.shape[0] for b in blocks)
    width, feats = weight.shape
    n = len(blocks)

    def body(_, *refs):
        parts, (w, b, joined, acts, mask, token) = refs[:n], refs[n:]
        token[...] = jnp.zeros_like(token)
        lay_rows(parts, joined)
        pre = jnp.dot(joined[...], w[...], preferred_element_type=F32) + b[...]
        acts[...] = jnp.maximum(pre, 0.0).astype(BF16)
        mask[...] = jnp.where(pre > 0, 1.0, 0.0).astype(BF16)

    return call(
        body,
        [((rows, width), BF16), ((rows, feats), BF16), ((rows, feats), BF16)],
        place,
        [*blocks, weight, bias],
        flops=2 * rows * width * feats,
    )


def fresh(x, edge):
    lane = lax.broadcasted_iota(jnp.int32, x.shape, 1)
    return jnp.where(lane >= edge, x, jnp.zeros_like(x))


def nt(a, b):
    return lax.dot_general(a, b, (((1,), (1,)), ((), ())), preferred_element_type=F32)


def nn(a, b):
    return jnp.dot(a, b, preferred_element_type=F32)


def decode(place, sources, weight, block):
    rows, feats = sources[0].shape
    half = rows // 2
    d = block
    wide = 4 * d
    e = d % 128

    def body(at_ref, *refs):
        a0, a1, a3, a2, b2, w, acts, keep, send, token = refs
        token[...] = jnp.zeros_like(token)
        for step, part in ((0, a0), (1, a1), (3, a3)):
            acts[lax.rem(at_ref[0] + step, 4)] = part[...]
        layer = lax.rem(at_ref[0] + 2, 4)
        acts[layer, :half, :] = a2[...]
        acts[layer, half:, :] = b2[...]
        for at, out in ((half, send), (0, keep)):
            a = [acts[s, at : at + half, :] for s in range(4)]
            out[:, : d - e] = nt(a[0], w[: d - e, :]).astype(BF16)
            part = nt(a[0], w[d - e : 2 * d, :]) + fresh(nt(a[1], w[4 * d - e : 5 * d, :]), e)
            out[:, d - e : 2 * d] = part.astype(BF16)
            part = (
                nt(a[0], w[2 * d : 3 * d - e, :])
                + nt(a[1], w[5 * d : 6 * d - e, :])
                + nt(a[2], w[7 * d : 8 * d - e, :])
            )
            out[:, 2 * d : 3 * d - e] = part.astype(BF16)
            part = (
                nt(a[0], w[3 * d - e : 4 * d, :])
                + nt(a[1], w[6 * d - e : 7 * d, :])
                + nt(a[2], w[8 * d - e : 9 * d, :])
                + fresh(nt(a[3], w[9 * d - e :, :]), e)
            )
            out[:, 3 * d - e :] = part.astype(BF16)

    return call(
        body,
        [((4, rows, feats), BF16), ((half, wide), BF16), ((half, wide), BF16)],
        place,
        [*sources, weight],
        flops=20 * rows * feats * d,
    )


def feature_grads(place, blocks, weight, block):
    rows = sum(b.shape[0] for b in blocks)
    feats = weight.shape[1]
    d = block
    e = d % 128
    half = rows // 2
    n = len(blocks)

    def body(at_ref, *refs):
        parts, (w, own, up, down, a1, b3, token, held, joined) = refs[:n], refs[n:]
        token[...] = jnp.zeros_like(token)
        lay_rows(parts, joined)

        def slot(layer):
            return lax.rem(layer + 4 - at_ref[0], 4)

        x = joined[...]
        held[slot(0)] = nn(x, w[: 4 * d, :]).astype(BF16)
        part = jnp.concatenate([fresh(x[:, d - e : d - e + 128], e), x[:, d - e + 128 :]], axis=1)
        held[slot(1)] = nn(part, w[4 * d - e : 7 * d, :]).astype(BF16)
        held[slot(2)] = nn(x[:, 2 * d :], w[7 * d : 9 * d, :]).astype(BF16)
        part = jnp.concatenate([fresh(x[:, 3 * d - e : 3 * d - e + 128], e), x[:, 3 * d - e + 128 :]], axis=1)
        held[slot(3)] = nn(part, w[9 * d - e :, :]).astype(BF16)
        own[...] = held[0]
        up[:half, :] = held[2, :half, :]
        up[half:, :] = held[1, half:, :]
        down[:half, :] = held[3, :half, :]
        down[half:, :] = held[2, half:, :]
        a1[...] = held[1, :half, :]
        b3[...] = held[3, half:, :]

    return call(
        body,
        [((rows, feats), BF16)] * 3 + [((half, feats), BF16)] * 2,
        place,
        [*blocks, weight],
        scratch=[((4, rows, feats), BF16), ((rows, 4 * d), BF16)],
        flops=20 * rows * feats * d,
    )


NEAR = ((0, 0), (1, 0), (0, 1), (0, 3))
FAR = ((1, 1), (1, 3), (0, 2), (1, 2))
PAIRS = tuple((s, t) for s in range(4) for t in range(s, 4))


def encoder_grad(place, rows, grads, mine, dtype):
    half, feats = rows[0].shape[1] // 2, grads[0].shape[1]

    def body(at_ref, r0, r1, g0, g1, out, token):
        token[...] = jnp.zeros_like(token)
        part = at_ref[1] if mine else 1 - at_ref[1]
        cut = pl.ds(pl.multiple_of(part * half, 128), half)
        out[...] = (nn(r0[:, cut].T, g0[...]) + nn(r1[:, cut].T, g1[...])).astype(dtype)

    flops = 4 * rows[0].shape[0] * half * feats
    return call(body, [((half, feats), dtype)], place, [*rows, *grads], flops=flops)[0]


def own_pairs_grad(place, acts, errors, other_acts, other_errors, block):
    _, rows, feats = acts[0].shape
    d = block
    wide = 4 * d
    tokens = other_errors.shape[1]
    count = 4 * rows
    own = len(PAIRS) // 2

    def body(at_ref, a0, a1, *refs):
        parts, (a2, others, out, total, token, turned, laid) = refs[: len(errors)], refs[len(errors) :]
        token[...] = jnp.zeros_like(token)
        at = 0
        for blocks in (NEAR, FAR):
            for core in range(2):
                for dx, dy in blocks:
                    x = lax.rem(at_ref[2] + dx, 2)
                    y = lax.rem(at_ref[3] + dy, 4)
                    c = lax.rem(at_ref[4] + core, 2)
                    laid[at : at + tokens, :] = others[(x * 4 + y) * 2 + c]
                    at += tokens
        sums = jnp.zeros((8, wide), F32)
        at = 0
        near, near_core, far, last, far_core, last_core = [part[...] for part in parts]
        far = jnp.concatenate([far, last], axis=0)
        far_core = jnp.concatenate([far_core, last_core], axis=0)
        for x in (near, near_core, far, far_core, laid[...]):
            size = x.shape[0]
            sums += nn(jnp.ones((8, size), BF16), x)
            for t in range(4):
                low = t * d // 128 * 128
                turned[t, :, at : at + size] = x[:, low : (t + 1) * d].T[t * d - low :]
            at += size
        total[...] = sums
        first = at_ref[1] == 0
        for i in range(own):
            s, t = [jnp.where(first, m, n) for m, n in zip(PAIRS[i], PAIRS[own + i])]
            part = nn(turned[t, :, :rows], a0[s]) + nn(turned[t, :, rows : 2 * rows], a1[s])
            out[i] = (part + nn(turned[t, :, 2 * rows :], a2[s])).astype(BF16)

    return call(
        body,
        [((own, d, feats), BF16), ((8, wide), F32)],
        place,
        [*acts, *errors, other_acts, other_errors],
        scratch=[((4, d, count), BF16), ((2 * rows, wide), BF16)],
        flops=10 * count * feats * d,
    )


def gather_rows(block, use):
    half = block.shape[0] // 2
    x1 = from_offset(block, X, 1)
    y1 = from_offset(block, Y, 1)
    y3 = from_offset(block, Y, -1)
    near = jnp.concatenate([block, x1, y1, y3], axis=0)
    near_core = from_offset(near, C, 1)
    xy1 = from_offset(y1, X, 1)
    xy3 = from_offset(x1, Y, -1)
    y2 = from_offset(y1, Y, 1)
    xy2a = from_offset(xy1[:half], Y, 1)
    xy2b = from_offset(xy3[half:], Y, -1)
    first, made = use([near, near_core])
    far = jnp.concatenate([xy1, xy3, y2], axis=0)
    far_core = from_offset(far, C, 1)
    last = jnp.concatenate(after([xy2a, xy2b], made), axis=0)
    last_core = from_offset(last, C, 1)
    return first, use([far, last, far_core, last_core])[0]


def sum_rows(near_after, far):
    rows = far[0].shape[0] // 4
    half = rows // 2

    def taken(pair, arrived, k):
        cut = slice(k * rows, (k + 1) * rows)
        return pair[cut].astype(F32) + arrived[cut].astype(F32)

    far_in = from_offset(far[1], C, 1)
    q11, q13, q02, q12 = [taken(far[0], far_in, k) for k in range(4)]
    a = to_offset(q12[:half].astype(BF16), Y, 1)
    b = to_offset(q12[half:].astype(BF16), Y, -1)
    near = near_after(a)
    near_in = from_offset(near[1], C, 1)
    q00, q10, q01, q03 = [taken(near[0], near_in, k) for k in range(4)]
    r02 = to_offset(q02.astype(BF16), Y, 1)
    r03 = to_offset(q03.astype(BF16), Y, -1)
    q11 = jnp.concatenate([q11[:half] + a.astype(F32), q11[half:]], axis=0)
    q13 = jnp.concatenate([q13[:half], q13[half:] + b.astype(F32)], axis=0)
    r11 = to_offset(q11.astype(BF16), X, 1)
    r13 = to_offset(q13.astype(BF16), Y, -1)
    q01 = q01 + r11.astype(F32) + r02.astype(F32)
    q10 = q10 + r13.astype(F32)
    r01 = to_offset(q01.astype(BF16), Y, 1)
    r10 = to_offset(q10.astype(BF16), X, 1)
    return q00, r03, r01, r10


def scaled_errors(place, parts, targets, bias, tokens):
    rows, layers, d = targets.shape

    def body(_, a, b, c, e, targets_ref, bias_ref, out, token):
        token[...] = jnp.zeros_like(token)
        total = a[...] + b[...].astype(F32) + c[...].astype(F32) + e[...].astype(F32)
        wanted = [targets_ref[:, t, :].astype(F32) - bias_ref[t : t + 1, :] for t in range(layers)]
        out[...] = ((total - jnp.concatenate(wanted, axis=1)) / tokens).astype(BF16)

    return call(body, [((rows, layers * d), BF16)], place, [*parts, targets, bias])[0]


def gather_layers(acts):
    half = acts.shape[0] // 2
    a1 = from_offset(acts, Z, 1)
    a3 = from_offset(acts, Z, -1)
    a2 = from_offset(a1[:half], Z, 1)
    b2 = from_offset(a3[half:], Z, -1)
    return acts, a1, a3, a2, b2


def sum_layers(own, up, down, a1, b3):
    half = a1.shape[0]
    up = to_offset(up, Z, 1)
    down = to_offset(down, Z, -1)
    gate = (up, down)
    a1 = to_offset((a1.astype(F32) + up[:half].astype(F32)).astype(BF16), Z, 1)
    b3 = to_offset((b3.astype(F32) + down[half:].astype(F32)).astype(BF16), Z, -1)
    first = own[:half].astype(F32) + a1.astype(F32) + down[:half].astype(F32)
    second = own[half:].astype(F32) + up[half:].astype(F32) + b3.astype(F32)
    return jnp.concatenate([first, second], axis=0), gate


def per_device(inputs, targets, enc_weight, enc_bias, dec_weight, dec_bias):
    layers, d = dec_bias.shape
    place = jnp.stack([lax.axis_index(axis) for axis in (Z, G, X, Y, C)]).astype(jnp.int32)
    tok_dev = inputs.shape[1]
    total_tokens = tok_dev * lax.axis_size(FEAT) * lax.axis_size(G)
    feats = dec_weight.shape[1]
    decoder = dec_weight.transpose(0, 2, 1).reshape(-1, feats)

    def forward(chunk):
        joined, acts, mask, _ = encode(place, chunk, enc_weight[0], enc_bias)
        sources = gather_layers(acts)
        return (joined, mask, sources), acts

    near, far = gather_rows(inputs[0], forward)
    other_acts = [from_offset(chunk[2][0], G, 1) for chunk in (near, far)]
    far_acts, *far_rows, _ = decode(after(place, *other_acts, *near[2][3:]), far[2], decoder, d)
    acts = []

    def near_after(*earlier):
        near_acts, *near_rows, _ = decode(after(place, *earlier), near[2], decoder, d)
        acts.extend([near_acts, far_acts])
        return near_rows

    parts = sum_rows(near_after, far_rows)
    scaled = scaled_errors(place, parts, targets, dec_bias, total_tokens)
    other_acts = lax.all_gather(jnp.concatenate(other_acts, axis=0), Z, axis=0)

    def backward(chunk):
        *parts, _ = feature_grads(place, chunk, decoder, d)
        dacts, gate = sum_layers(*parts)
        return (chunk, dacts, gate, parts[0]), parts[0]

    graded = gather_rows(scaled, backward)
    other_errors = from_offset(scaled, G, 1)
    other_errors = lax.all_gather(after(other_errors, *graded[1][0][2:], other_acts), FEAT, axis=0)
    dpre = [jnp.where(c[1] > 0, g[1], jnp.zeros_like(g[1])) for c, g in zip((near, far), graded)]
    enc_bias_grad = sum(jnp.sum(x, axis=0) for x in dpre)
    dpre = [x.astype(BF16) for x in dpre]
    rows = [near[0], far[0]]
    sent = encoder_grad(place, rows, dpre, False, BF16)
    kept = encoder_grad(after(place, sent), rows, dpre, True, F32)
    other_bias_grad = from_offset(enc_bias_grad, G, 1)
    own_errors = [*graded[0][0], *graded[1][0]]
    dec_grad, error_sums, _ = own_pairs_grad(after(place, sent), acts, own_errors, other_acts, other_errors, d)
    enc_grad = (kept + after(from_offset(sent, G, 1), error_sums).astype(F32)).astype(BF16)
    enc_bias_grad = enc_bias_grad + after(other_bias_grad, error_sums)
    return (
        enc_grad[None],
        enc_bias_grad[None],
        dec_grad.transpose(0, 2, 1),
        error_sums[0].reshape(layers, d),
    )


def solution(mesh):
    finer = Mesh(
        mesh.devices.reshape(mesh.shape["grp"], mesh.shape["layer"], 2, 4, 2),
        (G, Z, X, Y, C),
    )
    return jax.shard_map(
        per_device,
        mesh=finer,
        in_specs=(
            P(Z, GRP_FEAT, None),
            P(GRP_FEAT, None, Z),
            P(Z, None, FEAT),
            P(Z, FEAT),
            P(None, FEAT, Z),
            P(None, Z),
        ),
        out_specs=(P(Z, G, FEAT), P(Z, FEAT), P(G, FEAT, Z), P(None, Z)),
        check_vma=False,
    )
```

```python
import jax
import jax.numpy as jnp
from jax import lax
from jax.experimental import pallas as pl
from jax.experimental.pallas import tpu as pltpu
from jax.sharding import Mesh
from jax.sharding import PartitionSpec as P

X, Y, C, Z, G = ("feat_0", "feat_1", "feat_2", "layer", "grp")
FEAT = (X, Y, C)
GRP_FEAT = (G, X, Y, C)
BF16, F32 = (jnp.bfloat16, jnp.float32)
VMEM = pl.BlockSpec(memory_space=pltpu.VMEM)
ANY = pl.BlockSpec(memory_space=pl.ANY)
SMEM = pl.BlockSpec(memory_space=pltpu.SMEM)


def from_offset(x, axis, offset):
    size = lax.axis_size(axis)
    return lax.ppermute(x, axis, [((i + offset) % size, i) for i in range(size)])


def to_offset(x, axis, offset):
    return from_offset(x, axis, -offset)


def after(x, *earlier):
    return lax.optimization_barrier((x, *earlier))[0]


def size_of(shape, dtype):
    count = jnp.dtype(dtype).itemsize
    for n in shape:
        count *= n
    return count


def call(body, outs, place, args, scratch=(), flops=0, wait=(), copies=0):
    outs = [*outs, ((8, 128), F32)]
    moved = sum(size_of(a.shape, a.dtype) for a in args) + sum(size_of(*o) for o in outs)
    held = moved + sum(size_of(*s) for s in scratch)
    first, last = 1 + len(args), 1 + len(args) + len(wait)
    sems = [pltpu.SemaphoreType.DMA((copies,))] if copies else []

    def run(*refs):
        body(*refs[:first], *refs[last:])

    return pl.pallas_call(
        run,
        out_shape=[jax.ShapeDtypeStruct(s, d) for s, d in outs],
        in_specs=[SMEM] + [ANY if copies else VMEM] * (len(args) + len(wait)),
        out_specs=[VMEM] * len(outs),
        scratch_shapes=[pltpu.VMEM(s, d) for s, d in scratch] + sems,
        cost_estimate=pl.CostEstimate(flops=flops, bytes_accessed=moved, transcendentals=0),
        compiler_params=pltpu.CompilerParams(vmem_limit_bytes=60 << 20 if copies else held + (4 << 20)),
    )(place, *args, *wait)


def lay_rows(parts, target):
    at = 0
    for part in parts:
        target[at : at + part.shape[0], :] = part[...]
        at += part.shape[0]


def encode(place, blocks, weight, bias):
    rows = sum(b.shape[0] for b in blocks)
    width, feats = weight.shape
    n = len(blocks)

    def body(_, *refs):
        parts, (w, b, joined, acts, mask, token) = refs[:n], refs[n:]
        token[...] = jnp.zeros_like(token)
        lay_rows(parts, joined)
        pre = jnp.dot(joined[...], w[...], preferred_element_type=F32) + b[...]
        acts[...] = jnp.maximum(pre, 0.0).astype(BF16)
        mask[...] = jnp.where(pre > 0, 1.0, 0.0).astype(BF16)

    return call(
        body,
        [((rows, width), BF16), ((rows, feats), BF16), ((rows, feats), BF16)],
        place,
        [*blocks, weight, bias],
        flops=2 * rows * width * feats,
    )


def fresh(x, edge):
    lane = lax.broadcasted_iota(jnp.int32, x.shape, 1)
    return jnp.where(lane >= edge, x, jnp.zeros_like(x))


def nt(a, b):
    return lax.dot_general(a, b, (((1,), (1,)), ((), ())), preferred_element_type=F32)


def nn(a, b):
    return jnp.dot(a, b, preferred_element_type=F32)


def decode(place, sources, weight, block, wait=()):
    rows, feats = sources[0].shape
    half = rows // 2
    d = block
    wide = 4 * d
    e = d % 128

    def body(at_ref, *refs):
        a0, a1, a3, a2, b2, w, acts, keep, send, token = refs
        token[...] = jnp.zeros_like(token)
        for step, part in ((0, a0), (1, a1), (3, a3)):
            acts[lax.rem(at_ref[0] + step, 4)] = part[...]
        layer = lax.rem(at_ref[0] + 2, 4)
        acts[layer, :half, :] = a2[...]
        acts[layer, half:, :] = b2[...]
        for at, out in ((half, send), (0, keep)):
            a = [acts[s, at : at + half, :] for s in range(4)]
            out[:, : d - e] = nt(a[0], w[: d - e, :]).astype(BF16)
            part = nt(a[0], w[d - e : 2 * d, :]) + fresh(nt(a[1], w[4 * d - e : 5 * d, :]), e)
            out[:, d - e : 2 * d] = part.astype(BF16)
            part = (
                nt(a[0], w[2 * d : 3 * d - e, :])
                + nt(a[1], w[5 * d : 6 * d - e, :])
                + nt(a[2], w[7 * d : 8 * d - e, :])
            )
            out[:, 2 * d : 3 * d - e] = part.astype(BF16)
            part = (
                nt(a[0], w[3 * d - e : 4 * d, :])
                + nt(a[1], w[6 * d - e : 7 * d, :])
                + nt(a[2], w[8 * d - e : 9 * d, :])
                + fresh(nt(a[3], w[9 * d - e :, :]), e)
            )
            out[:, 3 * d - e :] = part.astype(BF16)

    return call(
        body,
        [((4, rows, feats), BF16), ((half, wide), BF16), ((half, wide), BF16)],
        place,
        [*sources, weight],
        flops=20 * rows * feats * d,
        wait=wait,
    )


def feature_grads(place, blocks, weight, block):
    rows = sum(b.shape[0] for b in blocks)
    feats = weight.shape[1]
    d = block
    e = d % 128
    half = rows // 2
    n = len(blocks)

    def body(at_ref, *refs):
        parts, (w, own, up, down, a1, b3, token, held, joined) = refs[:n], refs[n:]
        token[...] = jnp.zeros_like(token)
        lay_rows(parts, joined)

        def slot(layer):
            return lax.rem(layer + 4 - at_ref[0], 4)

        x = joined[...]
        held[slot(0)] = nn(x, w[: 4 * d, :]).astype(BF16)
        part = jnp.concatenate([fresh(x[:, d - e : d - e + 128], e), x[:, d - e + 128 :]], axis=1)
        held[slot(1)] = nn(part, w[4 * d - e : 7 * d, :]).astype(BF16)
        held[slot(2)] = nn(x[:, 2 * d :], w[7 * d : 9 * d, :]).astype(BF16)
        part = jnp.concatenate([fresh(x[:, 3 * d - e : 3 * d - e + 128], e), x[:, 3 * d - e + 128 :]], axis=1)
        held[slot(3)] = nn(part, w[9 * d - e :, :]).astype(BF16)
        own[...] = held[0]
        up[:half, :] = held[2, :half, :]
        up[half:, :] = held[1, half:, :]
        down[:half, :] = held[3, :half, :]
        down[half:, :] = held[2, half:, :]
        a1[...] = held[1, :half, :]
        b3[...] = held[3, half:, :]

    return call(
        body,
        [((rows, feats), BF16)] * 3 + [((half, feats), BF16)] * 2,
        place,
        [*blocks, weight],
        scratch=[((4, rows, feats), BF16), ((rows, 4 * d), BF16)],
        flops=20 * rows * feats * d,
    )


NEAR = ((0, 0), (1, 0), (0, 1), (0, 3))
FAR = ((1, 1), (1, 3), (0, 2), (1, 2))
PAIRS = tuple((s, t) for s in range(4) for t in range(s, 4))


def encoder_grad(place, rows, grads, mine, dtype):
    half, feats = rows[0].shape[1] // 2, grads[0].shape[1]

    def body(at_ref, r0, r1, g0, g1, out, token):
        token[...] = jnp.zeros_like(token)
        part = at_ref[1] if mine else 1 - at_ref[1]
        cut = pl.ds(pl.multiple_of(part * half, 128), half)
        out[...] = (nn(r0[:, cut].T, g0[...]) + nn(r1[:, cut].T, g1[...])).astype(dtype)

    flops = 4 * rows[0].shape[0] * half * feats
    return call(body, [((half, feats), dtype)], place, [*rows, *grads], flops=flops)[0]


def own_pairs_grad(place, acts, errors, other_acts, other_errors, block):
    _, rows, feats = acts[0].shape
    d = block
    wide = 4 * d
    count = 2 * rows
    tokens = other_errors.shape[1]
    own = len(PAIRS) // 2
    pieces, blocks = len(errors), other_errors.shape[0]
    copies = pieces + blocks + 3

    def body(at_ref, a0, a1, *refs):
        parts, refs = refs[:pieces], refs[pieces:]
        a2, others, out, total, token, turned, here, there, acts_here, acts_there, sems = refs
        token[...] = jnp.zeros_like(token)
        first, second, third, at = [], [], [], 0
        for part in parts:
            first.append((part, here.at[pl.ds(at, part.shape[0])]))
            at += part.shape[0]
        at = 0
        for chunk in (NEAR, FAR):
            for core in range(2):
                for dx, dy in chunk:
                    x = lax.rem(at_ref[2] + dx, 2)
                    y = lax.rem(at_ref[3] + dy, 4)
                    c = lax.rem(at_ref[4] + core, 2)
                    second.append((others.at[(x * 4 + y) * 2 + c], there.at[pl.ds(at, tokens)]))
                    at += tokens
        third.append((a0, acts_here.at[:, pl.ds(0, rows)]))
        third.append((a1, acts_here.at[:, pl.ds(rows, rows)]))
        third.append((a2, acts_there))
        moves = [pltpu.make_async_copy(*m, sems.at[k]) for k, m in enumerate(first + second + third)]
        for move in moves:
            move.start()
        sums = jnp.zeros((8, wide), F32)
        cuts = (moves[:pieces], moves[pieces : pieces + blocks])
        for k, (x_ref, awaited) in enumerate(zip((here, there), cuts)):
            for move in awaited:
                move.wait()
            for at in range(0, count, rows):
                x = x_ref[at : at + rows, :]
                sums += nn(jnp.ones((8, rows), BF16), x)
                for t in range(4):
                    low = t * d // 128 * 128
                    start = k * count + at
                    turned[t, :, start : start + rows] = x[:, low : (t + 1) * d].T[t * d - low :]
        total[...] = sums
        for move in moves[pieces + blocks :]:
            move.wait()
        mine = at_ref[1] == 0
        for i in range(own):
            s, t = [jnp.where(mine, m, n) for m, n in zip(PAIRS[i], PAIRS[own + i])]
            part = nn(turned[t, :, :count], acts_here[s]) + nn(turned[t, :, count:], acts_there[s])
            out[i] = part.astype(BF16)

    return call(
        body,
        [((own, d, feats), BF16), ((8, wide), F32)],
        place,
        [*acts, *errors, other_acts, other_errors],
        scratch=[((4, d, 2 * count), BF16)] + [((count, wide), BF16)] * 2 + [((4, count, feats), BF16)] * 2,
        flops=20 * count * feats * d,
        copies=copies,
    )


def gather_rows(block, use):
    half = block.shape[0] // 2
    x1 = from_offset(block, X, 1)
    y1 = from_offset(block, Y, 1)
    y3 = from_offset(block, Y, -1)
    near = jnp.concatenate([block, x1, y1, y3], axis=0)
    near_core = from_offset(near, C, 1)
    xy1 = from_offset(y1, X, 1)
    xy3 = from_offset(x1, Y, -1)
    y2 = from_offset(y1, Y, 1)
    xy2a = from_offset(xy1[:half], Y, 1)
    xy2b = from_offset(xy3[half:], Y, -1)
    first, made = use([near, near_core])
    far = jnp.concatenate([xy1, xy3, y2], axis=0)
    far_core = from_offset(far, C, 1)
    last = jnp.concatenate(after([xy2a, xy2b], made), axis=0)
    last_core = from_offset(last, C, 1)
    return first, use([far, last, far_core, last_core])[0]


def sum_rows(near_after, far):
    rows = far[0].shape[0] // 4
    half = rows // 2

    def taken(pair, arrived, k):
        cut = slice(k * rows, (k + 1) * rows)
        return pair[cut].astype(F32) + arrived[cut].astype(F32)

    far_in = from_offset(far[1], C, 1)
    q11, q13, q02, q12 = [taken(far[0], far_in, k) for k in range(4)]
    a = to_offset(q12[:half].astype(BF16), Y, 1)
    b = to_offset(q12[half:].astype(BF16), Y, -1)
    q11 = jnp.concatenate([q11[:half] + a.astype(F32), q11[half:]], axis=0).astype(BF16)
    q13 = jnp.concatenate([q13[:half], q13[half:] + b.astype(F32)], axis=0).astype(BF16)
    near = near_after(a)
    near_in = from_offset(near[1], C, 1)
    q00, q10, q01, q03 = [taken(near[0], near_in, k) for k in range(4)]
    r02 = to_offset(q02.astype(BF16), Y, 1)
    r11 = to_offset(q11, X, 1)
    r13 = to_offset(q13, Y, -1)
    r03 = to_offset(q03.astype(BF16), Y, -1)
    q01 = q01 + r11.astype(F32) + r02.astype(F32)
    q10 = q10 + r13.astype(F32)
    r01 = to_offset(q01.astype(BF16), Y, 1)
    r10 = to_offset(q10.astype(BF16), X, 1)
    return q00, r03, r01, r10


def scaled_errors(place, parts, targets, bias, tokens):
    rows, layers, d = targets.shape

    def body(_, a, b, c, e, targets_ref, bias_ref, out, token):
        token[...] = jnp.zeros_like(token)
        total = a[...] + b[...].astype(F32) + c[...].astype(F32) + e[...].astype(F32)
        wanted = [targets_ref[:, t, :].astype(F32) - bias_ref[t : t + 1, :] for t in range(layers)]
        out[...] = ((total - jnp.concatenate(wanted, axis=1)) / tokens).astype(BF16)

    return call(body, [((rows, layers * d), BF16)], place, [*parts, targets, bias])[0]


def gather_layers(acts):
    half = acts.shape[0] // 2
    a1 = from_offset(acts, Z, 1)
    a3 = from_offset(acts, Z, -1)
    a2 = from_offset(a1[:half], Z, 1)
    b2 = from_offset(a3[half:], Z, -1)
    return acts, a1, a3, a2, b2


def sum_layers(own, up, down, a1, b3):
    half = a1.shape[0]
    up = to_offset(up, Z, 1)
    down = to_offset(down, Z, -1)
    gate = (up, down)
    a1 = to_offset((a1.astype(F32) + up[:half].astype(F32)).astype(BF16), Z, 1)
    b3 = to_offset((b3.astype(F32) + down[half:].astype(F32)).astype(BF16), Z, -1)
    first = own[:half].astype(F32) + a1.astype(F32) + down[:half].astype(F32)
    second = own[half:].astype(F32) + up[half:].astype(F32) + b3.astype(F32)
    return jnp.concatenate([first, second], axis=0), gate


def per_device(inputs, targets, enc_weight, enc_bias, dec_weight, dec_bias):
    layers, d = dec_bias.shape
    place = jnp.stack([lax.axis_index(axis) for axis in (Z, G, X, Y, C)]).astype(jnp.int32)
    tok_dev = inputs.shape[1]
    total_tokens = tok_dev * lax.axis_size(FEAT) * lax.axis_size(G)
    feats = dec_weight.shape[1]
    decoder = dec_weight.transpose(0, 2, 1).reshape(-1, feats)

    def forward(chunk):
        joined, acts, mask, _ = encode(place, chunk, enc_weight[0], enc_bias)
        sources = gather_layers(acts)
        return (joined, mask, sources), acts

    near, far = gather_rows(inputs[0], forward)
    other_acts = [from_offset(chunk[2][0], G, 1) for chunk in (near, far)]
    far_acts, *far_rows, _ = decode(after(place, *other_acts, *near[2][3:]), far[2], decoder, d)
    acts = []

    def near_after(*earlier):
        near_acts, *near_rows, _ = decode(after(place, *earlier), near[2], decoder, d)
        acts.extend([near_acts, far_acts])
        return near_rows

    parts = sum_rows(near_after, far_rows)
    scaled = scaled_errors(place, parts, targets, dec_bias, total_tokens)
    other_acts = lax.all_gather(jnp.concatenate(other_acts, axis=0), Z, axis=0)

    def backward(chunk):
        *parts, _ = feature_grads(place, chunk, decoder, d)
        dacts, gate = sum_layers(*parts)
        return (chunk, dacts, gate, parts[0]), parts[0]

    graded = gather_rows(scaled, backward)
    other_errors = from_offset(scaled, G, 1)
    other_errors = lax.all_gather(after(other_errors, *graded[1][0][2:], other_acts), FEAT, axis=0)
    dpre = [jnp.where(c[1] > 0, g[1], jnp.zeros_like(g[1])) for c, g in zip((near, far), graded)]
    enc_bias_grad = sum(jnp.sum(x, axis=0) for x in dpre)
    dpre = [x.astype(BF16) for x in dpre]
    rows = [near[0], far[0]]
    sent = encoder_grad(place, rows, dpre, False, BF16)
    kept = encoder_grad(after(place, sent), rows, dpre, True, F32)
    other_bias_grad = from_offset(enc_bias_grad, G, 1)
    own_errors = [*graded[0][0], *graded[1][0]]
    dec_grad, error_sums, _ = own_pairs_grad(after(place, sent), acts, own_errors, other_acts, other_errors, d)
    enc_grad = (kept + after(from_offset(sent, G, 1), error_sums).astype(F32)).astype(BF16)
    enc_bias_grad = enc_bias_grad + after(other_bias_grad, error_sums)
    return (
        enc_grad[None],
        enc_bias_grad[None],
        dec_grad.transpose(0, 2, 1),
        error_sums[0].reshape(layers, d),
    )


def solution(mesh):
    finer = Mesh(
        mesh.devices.reshape(mesh.shape["grp"], mesh.shape["layer"], 2, 4, 2),
        (G, Z, X, Y, C),
    )
    return jax.shard_map(
        per_device,
        mesh=finer,
        in_specs=(
            P(Z, GRP_FEAT, None),
            P(GRP_FEAT, None, Z),
            P(Z, None, FEAT),
            P(Z, FEAT),
            P(None, FEAT, Z),
            P(None, Z),
        ),
        out_specs=(P(Z, G, FEAT), P(Z, FEAT), P(G, FEAT, Z), P(None, Z)),
        check_vma=False,
    )
```

```python
import jax
import jax.numpy as jnp
from jax import lax
from jax.experimental import pallas as pl
from jax.experimental.pallas import tpu as pltpu
from jax.sharding import Mesh
from jax.sharding import PartitionSpec as P

X, Y, C, Z, G = ("feat_0", "feat_1", "feat_2", "layer", "grp")
FEAT = (X, Y, C)
GRP_FEAT = (G, X, Y, C)
BF16, F32 = (jnp.bfloat16, jnp.float32)
VMEM = pl.BlockSpec(memory_space=pltpu.VMEM)
ANY = pl.BlockSpec(memory_space=pl.ANY)
SMEM = pl.BlockSpec(memory_space=pltpu.SMEM)


def from_offset(x, axis, offset):
    size = lax.axis_size(axis)
    return lax.ppermute(x, axis, [((i + offset) % size, i) for i in range(size)])


def to_offset(x, axis, offset):
    return from_offset(x, axis, -offset)


def after(x, *earlier):
    return lax.optimization_barrier((x, *earlier))[0]


def size_of(shape, dtype):
    count = jnp.dtype(dtype).itemsize
    for n in shape:
        count *= n
    return count


def call(body, outs, place, args, scratch=(), flops=0, wait=(), copies=0):
    outs = [*outs, ((8, 128), F32)]
    moved = sum(size_of(a.shape, a.dtype) for a in args) + sum(size_of(*o) for o in outs)
    held = moved + sum(size_of(*s) for s in scratch)
    first, last = 1 + len(args), 1 + len(args) + len(wait)
    sems = [pltpu.SemaphoreType.DMA((copies,))] if copies else []

    def run(*refs):
        body(*refs[:first], *refs[last:])

    return pl.pallas_call(
        run,
        out_shape=[jax.ShapeDtypeStruct(s, d) for s, d in outs],
        in_specs=[SMEM] + [ANY if copies else VMEM] * (len(args) + len(wait)),
        out_specs=[VMEM] * len(outs),
        scratch_shapes=[pltpu.VMEM(s, d) for s, d in scratch] + sems,
        cost_estimate=pl.CostEstimate(flops=flops, bytes_accessed=moved, transcendentals=0),
        compiler_params=pltpu.CompilerParams(vmem_limit_bytes=60 << 20 if copies else held + (4 << 20)),
    )(place, *args, *wait)


def lay_rows(parts, target):
    at = 0
    for part in parts:
        target[at : at + part.shape[0], :] = part[...]
        at += part.shape[0]


def encode(place, blocks, weight, bias):
    rows = sum(b.shape[0] for b in blocks)
    width, feats = weight.shape
    n = len(blocks)

    def body(_, *refs):
        parts, (w, b, joined, acts, mask, token) = refs[:n], refs[n:]
        token[...] = jnp.zeros_like(token)
        lay_rows(parts, joined)
        pre = jnp.dot(joined[...], w[...], preferred_element_type=F32) + b[...]
        acts[...] = jnp.maximum(pre, 0.0).astype(BF16)
        mask[...] = jnp.where(pre > 0, 1.0, 0.0).astype(BF16)

    return call(
        body,
        [((rows, width), BF16), ((rows, feats), BF16), ((rows, feats), BF16)],
        place,
        [*blocks, weight, bias],
        flops=2 * rows * width * feats,
    )


def fresh(x, edge):
    lane = lax.broadcasted_iota(jnp.int32, x.shape, 1)
    return jnp.where(lane >= edge, x, jnp.zeros_like(x))


def nt(a, b):
    return lax.dot_general(a, b, (((1,), (1,)), ((), ())), preferred_element_type=F32)


def nn(a, b):
    return jnp.dot(a, b, preferred_element_type=F32)


def decode(place, sources, weight, block, wait=()):
    rows, feats = sources[0].shape
    half = rows // 2
    d = block
    wide = 4 * d
    e = d % 128

    def body(at_ref, *refs):
        a0, a1, a3, a2, b2, w, acts, keep, send, token = refs
        token[...] = jnp.zeros_like(token)
        for step, part in ((0, a0), (1, a1), (3, a3)):
            acts[lax.rem(at_ref[0] + step, 4)] = part[...]
        layer = lax.rem(at_ref[0] + 2, 4)
        acts[layer, :half, :] = a2[...]
        acts[layer, half:, :] = b2[...]
        for at, out in ((half, send), (0, keep)):
            a = [acts[s, at : at + half, :] for s in range(4)]
            out[:, : d - e] = nt(a[0], w[: d - e, :]).astype(BF16)
            part = nt(a[0], w[d - e : 2 * d, :]) + fresh(nt(a[1], w[4 * d - e : 5 * d, :]), e)
            out[:, d - e : 2 * d] = part.astype(BF16)
            part = (
                nt(a[0], w[2 * d : 3 * d - e, :])
                + nt(a[1], w[5 * d : 6 * d - e, :])
                + nt(a[2], w[7 * d : 8 * d - e, :])
            )
            out[:, 2 * d : 3 * d - e] = part.astype(BF16)
            part = (
                nt(a[0], w[3 * d - e : 4 * d, :])
                + nt(a[1], w[6 * d - e : 7 * d, :])
                + nt(a[2], w[8 * d - e : 9 * d, :])
                + fresh(nt(a[3], w[9 * d - e :, :]), e)
            )
            out[:, 3 * d - e :] = part.astype(BF16)

    return call(
        body,
        [((4, rows, feats), BF16), ((half, wide), BF16), ((half, wide), BF16)],
        place,
        [*sources, weight],
        flops=20 * rows * feats * d,
        wait=wait,
    )


def feature_grads(place, blocks, weight, block):
    rows = sum(b.shape[0] for b in blocks)
    feats = weight.shape[1]
    d = block
    e = d % 128
    half = rows // 2
    n = len(blocks)

    def body(at_ref, *refs):
        parts, (w, own, up, down, a1, b3, token, held, joined) = refs[:n], refs[n:]
        token[...] = jnp.zeros_like(token)
        lay_rows(parts, joined)

        def slot(layer):
            return lax.rem(layer + 4 - at_ref[0], 4)

        x = joined[...]
        held[slot(0)] = nn(x, w[: 4 * d, :]).astype(BF16)
        part = jnp.concatenate([fresh(x[:, d - e : d - e + 128], e), x[:, d - e + 128 :]], axis=1)
        held[slot(1)] = nn(part, w[4 * d - e : 7 * d, :]).astype(BF16)
        held[slot(2)] = nn(x[:, 2 * d :], w[7 * d : 9 * d, :]).astype(BF16)
        part = jnp.concatenate([fresh(x[:, 3 * d - e : 3 * d - e + 128], e), x[:, 3 * d - e + 128 :]], axis=1)
        held[slot(3)] = nn(part, w[9 * d - e :, :]).astype(BF16)
        own[...] = held[0]
        up[:half, :] = held[2, :half, :]
        up[half:, :] = held[1, half:, :]
        down[:half, :] = held[3, :half, :]
        down[half:, :] = held[2, half:, :]
        a1[...] = held[1, :half, :]
        b3[...] = held[3, half:, :]

    return call(
        body,
        [((rows, feats), BF16)] * 3 + [((half, feats), BF16)] * 2,
        place,
        [*blocks, weight],
        scratch=[((4, rows, feats), BF16), ((rows, 4 * d), BF16)],
        flops=20 * rows * feats * d,
    )


NEAR = ((0, 0), (1, 0), (0, 1), (0, 3))
FAR = ((1, 1), (1, 3), (0, 2), (1, 2))
PAIRS = tuple((s, t) for s in range(4) for t in range(s, 4))


def encoder_grad(place, rows, grads, mine, dtype):
    half, feats = rows[0].shape[1] // 2, grads[0].shape[1]

    def body(at_ref, r0, r1, g0, g1, out, token):
        token[...] = jnp.zeros_like(token)
        part = at_ref[1] if mine else 1 - at_ref[1]
        cut = pl.ds(pl.multiple_of(part * half, 128), half)
        out[...] = (nn(r0[:, cut].T, g0[...]) + nn(r1[:, cut].T, g1[...])).astype(dtype)

    flops = 4 * rows[0].shape[0] * half * feats
    return call(body, [((half, feats), dtype)], place, [*rows, *grads], flops=flops)[0]


def own_pairs_grad(place, acts, errors, other_acts, other_errors, block):
    _, rows, feats = acts[0].shape
    d = block
    wide = 4 * d
    count = 2 * rows
    tokens = other_errors.shape[1]
    own = len(PAIRS) // 2
    pieces, blocks = len(errors), other_errors.shape[0]
    copies = pieces + blocks + 3

    def body(at_ref, a0, a1, *refs):
        parts, refs = refs[:pieces], refs[pieces:]
        a2, others, out, total, token, turned, here, there, acts_here, acts_there, sems = refs
        token[...] = jnp.zeros_like(token)
        first, second, third, at = [], [], [], 0
        for part in parts:
            first.append((part, here.at[pl.ds(at, part.shape[0])]))
            at += part.shape[0]
        at = 0
        for chunk in (NEAR, FAR):
            for core in range(2):
                for dx, dy in chunk:
                    x = lax.rem(at_ref[2] + dx, 2)
                    y = lax.rem(at_ref[3] + dy, 4)
                    c = lax.rem(at_ref[4] + core, 2)
                    second.append((others.at[(x * 4 + y) * 2 + c], there.at[pl.ds(at, tokens)]))
                    at += tokens
        third.append((a0, acts_here.at[:, pl.ds(0, rows)]))
        third.append((a1, acts_here.at[:, pl.ds(rows, rows)]))
        third.append((a2, acts_there))
        moves = [pltpu.make_async_copy(*m, sems.at[k]) for k, m in enumerate(first + second + third)]
        for move in moves:
            move.start()
        sums = jnp.zeros((8, wide), F32)
        cuts = (moves[:pieces], moves[pieces : pieces + blocks])
        for k, (x_ref, awaited) in enumerate(zip((here, there), cuts)):
            for move in awaited:
                move.wait()
            for at in range(0, count, rows):
                x = x_ref[at : at + rows, :]
                sums += nn(jnp.ones((8, rows), BF16), x)
                for t in range(4):
                    low = t * d // 128 * 128
                    start = k * count + at
                    turned[t, :, start : start + rows] = x[:, low : (t + 1) * d].T[t * d - low :]
        total[...] = sums
        for move in moves[pieces + blocks :]:
            move.wait()
        mine = at_ref[1] == 0
        for i in range(own):
            s, t = [jnp.where(mine, m, n) for m, n in zip(PAIRS[i], PAIRS[own + i])]
            part = nn(turned[t, :, :count], acts_here[s]) + nn(turned[t, :, count:], acts_there[s])
            out[i] = part.astype(BF16)

    return call(
        body,
        [((own, d, feats), BF16), ((8, wide), F32)],
        place,
        [*acts, *errors, other_acts, other_errors],
        scratch=[((4, d, 2 * count), BF16)] + [((count, wide), BF16)] * 2 + [((4, count, feats), BF16)] * 2,
        flops=20 * count * feats * d,
        copies=copies,
    )


def gather_rows(block, use):
    x1 = from_offset(block, X, 1)
    y1 = from_offset(block, Y, 1)
    y3 = from_offset(block, Y, -1)
    near = jnp.concatenate([block, x1, y1, y3], axis=0)
    near_core = from_offset(near, C, 1)
    xy1 = from_offset(y1, X, 1)
    xy3 = from_offset(x1, Y, -1)
    y2 = from_offset(y1, Y, 1)
    xy2 = from_offset(xy1, Y, 1)
    first, made = use([near, near_core])
    y2, xy2 = after((y2, xy2), made)
    far = jnp.concatenate([xy1, xy3, y2], axis=0)
    far_core = from_offset(far, C, 1)
    xy2_core = from_offset(xy2, C, 1)
    return first, use([far, xy2, far_core, xy2_core])[0]


def sum_rows(near_after, far):
    rows = far[0].shape[0] // 4

    def taken(pair, arrived, k):
        cut = slice(k * rows, (k + 1) * rows)
        return pair[cut].astype(F32) + arrived[cut].astype(F32)

    far_in = from_offset(far[1], C, 1)
    q11, q13, q02, q12 = [taken(far[0], far_in, k) for k in range(4)]
    r12 = to_offset(q12.astype(BF16), Y, 1)
    r13 = to_offset(q13.astype(BF16), Y, -1)
    r02 = to_offset(q02.astype(BF16), Y, 1)
    near = near_after()
    near_in = from_offset(near[1], C, 1)
    q00, q10, q01, q03 = [taken(near[0], near_in, k) for k in range(4)]
    r11 = to_offset((q11 + r12.astype(F32)).astype(BF16), X, 1)
    r03 = to_offset(q03.astype(BF16), Y, -1)
    q01 = q01 + r11.astype(F32) + r02.astype(F32)
    q10 = q10 + r13.astype(F32)
    r01 = to_offset(q01.astype(BF16), Y, 1)
    r10 = to_offset(q10.astype(BF16), X, 1)
    return q00, r03, r01, r10


def scaled_errors(place, parts, targets, bias, tokens):
    rows, layers, d = targets.shape

    def body(_, a, b, c, e, targets_ref, bias_ref, out, token):
        token[...] = jnp.zeros_like(token)
        total = a[...] + b[...].astype(F32) + c[...].astype(F32) + e[...].astype(F32)
        wanted = [targets_ref[:, t, :].astype(F32) - bias_ref[t : t + 1, :] for t in range(layers)]
        out[...] = ((total - jnp.concatenate(wanted, axis=1)) / tokens).astype(BF16)

    return call(body, [((rows, layers * d), BF16)], place, [*parts, targets, bias])[0]


def gather_layers(acts):
    half = acts.shape[0] // 2
    a1 = from_offset(acts, Z, 1)
    a3 = from_offset(acts, Z, -1)
    a2 = from_offset(a1[:half], Z, 1)
    b2 = from_offset(a3[half:], Z, -1)
    return acts, a1, a3, a2, b2


def sum_layers(own, up, down, a1, b3):
    half = a1.shape[0]
    up = to_offset(up, Z, 1)
    down = to_offset(down, Z, -1)
    gate = (up, down)
    a1 = to_offset((a1.astype(F32) + up[:half].astype(F32)).astype(BF16), Z, 1)
    b3 = to_offset((b3.astype(F32) + down[half:].astype(F32)).astype(BF16), Z, -1)
    first = own[:half].astype(F32) + a1.astype(F32) + down[:half].astype(F32)
    second = own[half:].astype(F32) + up[half:].astype(F32) + b3.astype(F32)
    return jnp.concatenate([first, second], axis=0), gate


def per_device(inputs, targets, enc_weight, enc_bias, dec_weight, dec_bias):
    layers, d = dec_bias.shape
    place = jnp.stack([lax.axis_index(axis) for axis in (Z, G, X, Y, C)]).astype(jnp.int32)
    tok_dev = inputs.shape[1]
    total_tokens = tok_dev * lax.axis_size(FEAT) * lax.axis_size(G)
    feats = dec_weight.shape[1]
    decoder = dec_weight.transpose(0, 2, 1).reshape(-1, feats)

    def forward(chunk):
        joined, acts, mask, _ = encode(place, chunk, enc_weight[0], enc_bias)
        sources = gather_layers(acts)
        return (joined, mask, sources), acts

    near, far = gather_rows(inputs[0], forward)
    other_acts = [from_offset(chunk[2][0], G, 1) for chunk in (near, far)]
    far_acts, *far_rows, token = decode(after(place, *other_acts, *near[2][3:]), far[2], decoder, d)
    acts = []

    def near_after():
        near_acts, *near_rows, _ = decode(place, near[2], decoder, d, (token,))
        acts.extend([near_acts, far_acts])
        return near_rows

    parts = sum_rows(near_after, far_rows)
    scaled = scaled_errors(place, parts, targets, dec_bias, total_tokens)
    other_acts = lax.all_gather(jnp.concatenate(other_acts, axis=0), Z, axis=0)

    def backward(chunk):
        *parts, _ = feature_grads(place, chunk, decoder, d)
        dacts, gate = sum_layers(*parts)
        return (chunk, dacts, gate, parts[0]), parts[0]

    graded = gather_rows(scaled, backward)
    other_errors = from_offset(after(scaled, graded[0][3]), G, 1)
    other_errors = lax.all_gather(after(other_errors, *graded[1][0][2:], other_acts), FEAT, axis=0)
    dpre = [jnp.where(c[1] > 0, g[1], jnp.zeros_like(g[1])) for c, g in zip((near, far), graded)]
    enc_bias_grad = sum(jnp.sum(x, axis=0) for x in dpre)
    dpre = [x.astype(BF16) for x in dpre]
    rows = [near[0], far[0]]
    sent = encoder_grad(place, rows, dpre, False, BF16)
    kept = encoder_grad(after(place, sent), rows, dpre, True, F32)
    other_bias_grad = from_offset(enc_bias_grad, G, 1)
    own_errors = [*graded[0][0], *graded[1][0]]
    dec_grad, error_sums, _ = own_pairs_grad(after(place, sent), acts, own_errors, other_acts, other_errors, d)
    enc_grad = (kept + after(from_offset(sent, G, 1), error_sums).astype(F32)).astype(BF16)
    enc_bias_grad = enc_bias_grad + after(other_bias_grad, error_sums)
    return (
        enc_grad[None],
        enc_bias_grad[None],
        dec_grad.transpose(0, 2, 1),
        error_sums[0].reshape(layers, d),
    )


def solution(mesh):
    finer = Mesh(
        mesh.devices.reshape(mesh.shape["grp"], mesh.shape["layer"], 2, 4, 2),
        (G, Z, X, Y, C),
    )
    return jax.shard_map(
        per_device,
        mesh=finer,
        in_specs=(
            P(Z, GRP_FEAT, None),
            P(GRP_FEAT, None, Z),
            P(Z, None, FEAT),
            P(Z, FEAT),
            P(None, FEAT, Z),
            P(None, Z),
        ),
        out_specs=(P(Z, G, FEAT), P(Z, FEAT), P(G, FEAT, Z), P(None, Z)),
        check_vma=False,
    )
```

```python
import jax
import jax.numpy as jnp
from jax import lax
from jax.experimental import pallas as pl
from jax.experimental.pallas import tpu as pltpu
from jax.sharding import Mesh
from jax.sharding import PartitionSpec as P

X, Y, C, Z, G = ("feat_0", "feat_1", "feat_2", "layer", "grp")
FEAT = (X, Y, C)
GRP_FEAT = (G, X, Y, C)
BF16, F32 = (jnp.bfloat16, jnp.float32)
VMEM = pl.BlockSpec(memory_space=pltpu.VMEM)
ANY = pl.BlockSpec(memory_space=pl.ANY)
SMEM = pl.BlockSpec(memory_space=pltpu.SMEM)


def from_offset(x, axis, offset):
    size = lax.axis_size(axis)
    return lax.ppermute(x, axis, [((i + offset) % size, i) for i in range(size)])


def to_offset(x, axis, offset):
    return from_offset(x, axis, -offset)


def after(x, *earlier):
    return lax.optimization_barrier((x, *earlier))[0]


def size_of(shape, dtype):
    count = jnp.dtype(dtype).itemsize
    for n in shape:
        count *= n
    return count


def call(body, outs, place, args, scratch=(), flops=0, wait=(), copies=0):
    outs = [*outs, ((8, 128), F32)]
    moved = sum(size_of(a.shape, a.dtype) for a in args) + sum(size_of(*o) for o in outs)
    held = moved + sum(size_of(*s) for s in scratch)
    first, last = 1 + len(args), 1 + len(args) + len(wait)
    sems = [pltpu.SemaphoreType.DMA((copies,))] if copies else []

    def run(*refs):
        body(*refs[:first], *refs[last:])

    return pl.pallas_call(
        run,
        out_shape=[jax.ShapeDtypeStruct(s, d) for s, d in outs],
        in_specs=[SMEM] + [ANY if copies else VMEM] * (len(args) + len(wait)),
        out_specs=[VMEM] * len(outs),
        scratch_shapes=[pltpu.VMEM(s, d) for s, d in scratch] + sems,
        cost_estimate=pl.CostEstimate(flops=flops, bytes_accessed=moved, transcendentals=0),
        compiler_params=pltpu.CompilerParams(vmem_limit_bytes=60 << 20 if copies else held + (4 << 20)),
    )(place, *args, *wait)


def lay_rows(parts, target):
    at = 0
    for part in parts:
        target[at : at + part.shape[0], :] = part[...]
        at += part.shape[0]


def encode(place, blocks, weight, bias):
    rows = sum(b.shape[0] for b in blocks)
    width, feats = weight.shape
    n = len(blocks)

    def body(_, *refs):
        parts, (w, b, joined, acts, mask, token) = refs[:n], refs[n:]
        token[...] = jnp.zeros_like(token)
        lay_rows(parts, joined)
        pre = jnp.dot(joined[...], w[...], preferred_element_type=F32) + b[...]
        acts[...] = jnp.maximum(pre, 0.0).astype(BF16)
        mask[...] = jnp.where(pre > 0, 1.0, 0.0).astype(BF16)

    return call(
        body,
        [((rows, width), BF16), ((rows, feats), BF16), ((rows, feats), BF16)],
        place,
        [*blocks, weight, bias],
        flops=2 * rows * width * feats,
    )


def fresh(x, edge):
    lane = lax.broadcasted_iota(jnp.int32, x.shape, 1)
    return jnp.where(lane >= edge, x, jnp.zeros_like(x))


def nt(a, b):
    return lax.dot_general(a, b, (((1,), (1,)), ((), ())), preferred_element_type=F32)


def nn(a, b):
    return jnp.dot(a, b, preferred_element_type=F32)


def decode(place, sources, weight, block, wait=()):
    rows, feats = sources[0].shape
    half = rows // 2
    d = block
    wide = 4 * d
    e = d % 128

    def body(at_ref, *refs):
        a0, a1, a3, a2, b2, w, acts, keep, send, token = refs
        token[...] = jnp.zeros_like(token)
        for step, part in ((0, a0), (1, a1), (3, a3)):
            acts[lax.rem(at_ref[0] + step, 4)] = part[...]
        layer = lax.rem(at_ref[0] + 2, 4)
        acts[layer, :half, :] = a2[...]
        acts[layer, half:, :] = b2[...]
        for at, out in ((half, send), (0, keep)):
            a = [acts[s, at : at + half, :] for s in range(4)]
            out[:, : d - e] = nt(a[0], w[: d - e, :]).astype(BF16)
            part = nt(a[0], w[d - e : 2 * d, :]) + fresh(nt(a[1], w[4 * d - e : 5 * d, :]), e)
            out[:, d - e : 2 * d] = part.astype(BF16)
            part = (
                nt(a[0], w[2 * d : 3 * d - e, :])
                + nt(a[1], w[5 * d : 6 * d - e, :])
                + nt(a[2], w[7 * d : 8 * d - e, :])
            )
            out[:, 2 * d : 3 * d - e] = part.astype(BF16)
            part = (
                nt(a[0], w[3 * d - e : 4 * d, :])
                + nt(a[1], w[6 * d - e : 7 * d, :])
                + nt(a[2], w[8 * d - e : 9 * d, :])
                + fresh(nt(a[3], w[9 * d - e :, :]), e)
            )
            out[:, 3 * d - e :] = part.astype(BF16)

    return call(
        body,
        [((4, rows, feats), BF16), ((half, wide), BF16), ((half, wide), BF16)],
        place,
        [*sources, weight],
        flops=20 * rows * feats * d,
        wait=wait,
    )


def feature_grads(place, blocks, weight, block):
    rows = sum(b.shape[0] for b in blocks)
    feats = weight.shape[1]
    d = block
    e = d % 128
    half = rows // 2
    n = len(blocks)

    def body(at_ref, *refs):
        parts, (w, own, up, down, a1, b3, token, held, joined) = refs[:n], refs[n:]
        token[...] = jnp.zeros_like(token)
        lay_rows(parts, joined)

        def slot(layer):
            return lax.rem(layer + 4 - at_ref[0], 4)

        x = joined[...]
        held[slot(0)] = nn(x, w[: 4 * d, :]).astype(BF16)
        part = jnp.concatenate([fresh(x[:, d - e : d - e + 128], e), x[:, d - e + 128 :]], axis=1)
        held[slot(1)] = nn(part, w[4 * d - e : 7 * d, :]).astype(BF16)
        held[slot(2)] = nn(x[:, 2 * d :], w[7 * d : 9 * d, :]).astype(BF16)
        part = jnp.concatenate([fresh(x[:, 3 * d - e : 3 * d - e + 128], e), x[:, 3 * d - e + 128 :]], axis=1)
        held[slot(3)] = nn(part, w[9 * d - e :, :]).astype(BF16)
        own[...] = held[0]
        up[:half, :] = held[2, :half, :]
        up[half:, :] = held[1, half:, :]
        down[:half, :] = held[3, :half, :]
        down[half:, :] = held[2, half:, :]
        a1[...] = held[1, :half, :]
        b3[...] = held[3, half:, :]

    return call(
        body,
        [((rows, feats), BF16)] * 3 + [((half, feats), BF16)] * 2,
        place,
        [*blocks, weight],
        scratch=[((4, rows, feats), BF16), ((rows, 4 * d), BF16)],
        flops=20 * rows * feats * d,
    )


NEAR = ((0, 0), (1, 0), (0, 1), (0, 3))
FAR = ((1, 1), (1, 3), (0, 2), (1, 2))
PAIRS = tuple((s, t) for s in range(4) for t in range(s, 4))


def encoder_grad(place, rows, grads, mine, dtype):
    half, feats = rows[0].shape[1] // 2, grads[0].shape[1]

    def body(at_ref, r0, r1, g0, g1, out, token):
        token[...] = jnp.zeros_like(token)
        part = at_ref[1] if mine else 1 - at_ref[1]
        cut = pl.ds(pl.multiple_of(part * half, 128), half)
        out[...] = (nn(r0[:, cut].T, g0[...]) + nn(r1[:, cut].T, g1[...])).astype(dtype)

    flops = 4 * rows[0].shape[0] * half * feats
    return call(body, [((half, feats), dtype)], place, [*rows, *grads], flops=flops)[0]


def own_pairs_grad(place, acts, errors, other_acts, other_errors, block):
    _, rows, feats = acts[0].shape
    d = block
    wide = 4 * d
    count = 2 * rows
    tokens = other_errors.shape[1]
    own = len(PAIRS) // 2
    pieces, blocks = len(errors), other_errors.shape[0]
    copies = pieces + blocks + 3

    def body(at_ref, a0, a1, *refs):
        parts, refs = refs[:pieces], refs[pieces:]
        a2, others, out, total, token, turned, here, there, acts_here, acts_there, sems = refs
        token[...] = jnp.zeros_like(token)
        first, second, third, at = [], [], [], 0
        for part in parts:
            first.append((part, here.at[pl.ds(at, part.shape[0])]))
            at += part.shape[0]
        at = 0
        for chunk in (NEAR, FAR):
            for core in range(2):
                for dx, dy in chunk:
                    x = lax.rem(at_ref[2] + dx, 2)
                    y = lax.rem(at_ref[3] + dy, 4)
                    c = lax.rem(at_ref[4] + core, 2)
                    second.append((others.at[(x * 4 + y) * 2 + c], there.at[pl.ds(at, tokens)]))
                    at += tokens
        third.append((a0, acts_here.at[:, pl.ds(0, rows)]))
        third.append((a1, acts_here.at[:, pl.ds(rows, rows)]))
        third.append((a2, acts_there))
        moves = [pltpu.make_async_copy(*m, sems.at[k]) for k, m in enumerate(first + second + third)]
        for move in moves:
            move.start()
        sums = jnp.zeros((8, wide), F32)
        cuts = (moves[:pieces], moves[pieces : pieces + blocks])
        for k, (x_ref, awaited) in enumerate(zip((here, there), cuts)):
            for move in awaited:
                move.wait()
            for at in range(0, count, rows):
                x = x_ref[at : at + rows, :]
                sums += nn(jnp.ones((8, rows), BF16), x)
                for t in range(4):
                    low = t * d // 128 * 128
                    start = k * count + at
                    turned[t, :, start : start + rows] = x[:, low : (t + 1) * d].T[t * d - low :]
        total[...] = sums
        for move in moves[pieces + blocks :]:
            move.wait()
        mine = at_ref[1] == 0
        for i in range(own):
            s, t = [jnp.where(mine, m, n) for m, n in zip(PAIRS[i], PAIRS[own + i])]
            part = nn(turned[t, :, :count], acts_here[s]) + nn(turned[t, :, count:], acts_there[s])
            out[i] = part.astype(BF16)

    return call(
        body,
        [((own, d, feats), BF16), ((8, wide), F32)],
        place,
        [*acts, *errors, other_acts, other_errors],
        scratch=[((4, d, 2 * count), BF16)] + [((count, wide), BF16)] * 2 + [((4, count, feats), BF16)] * 2,
        flops=20 * count * feats * d,
        copies=copies,
    )


def gather_rows(block, use, also=()):
    x1 = from_offset(block, X, 1)
    y1 = from_offset(block, Y, 1)
    y3 = from_offset(block, Y, -1)
    near = jnp.concatenate([block, x1, y1, y3], axis=0)
    near_core = from_offset(near, C, 1)
    xy1 = from_offset(y1, X, 1)
    xy3 = from_offset(x1, Y, -1)
    y2 = from_offset(y1, Y, 1)
    xy2 = from_offset(xy1, Y, 1)
    first, made = use([near, near_core])
    y2, xy2 = after((y2, xy2), made, *also)
    far = jnp.concatenate([xy1, xy3, y2], axis=0)
    far_core = from_offset(far, C, 1)
    xy2_core = from_offset(xy2, C, 1)
    return first, use([far, xy2, far_core, xy2_core])[0]


def sum_rows(near_after, far):
    rows = far[0].shape[0] // 4

    def taken(pair, arrived, k):
        cut = slice(k * rows, (k + 1) * rows)
        return pair[cut].astype(F32) + arrived[cut].astype(F32)

    far_in = from_offset(far[1], C, 1)
    q11, q13, q02, q12 = [taken(far[0], far_in, k) for k in range(4)]
    r12 = to_offset(q12.astype(BF16), Y, 1)
    r13 = to_offset(q13.astype(BF16), Y, -1)
    r02 = to_offset(q02.astype(BF16), Y, 1)
    near = near_after()
    near_in = from_offset(near[1], C, 1)
    q00, q10, q01, q03 = [taken(near[0], near_in, k) for k in range(4)]
    r11 = to_offset((q11 + r12.astype(F32)).astype(BF16), X, 1)
    r03 = to_offset(q03.astype(BF16), Y, -1)
    q01 = q01 + r11.astype(F32) + r02.astype(F32)
    q10 = q10 + r13.astype(F32)
    r01 = to_offset(q01.astype(BF16), Y, 1)
    r10 = to_offset(q10.astype(BF16), X, 1)
    return q00, r03, r01, r10


def scaled_errors(place, parts, targets, bias, tokens):
    rows, layers, d = targets.shape

    def body(_, a, b, c, e, targets_ref, bias_ref, out, token):
        token[...] = jnp.zeros_like(token)
        total = a[...] + b[...].astype(F32) + c[...].astype(F32) + e[...].astype(F32)
        wanted = [targets_ref[:, t, :].astype(F32) - bias_ref[t : t + 1, :] for t in range(layers)]
        out[...] = ((total - jnp.concatenate(wanted, axis=1)) / tokens).astype(BF16)

    return call(body, [((rows, layers * d), BF16)], place, [*parts, targets, bias])[0]


def gather_layers(acts):
    half = acts.shape[0] // 2
    a1 = from_offset(acts, Z, 1)
    a3 = from_offset(acts, Z, -1)
    a2 = from_offset(a1[:half], Z, 1)
    b2 = from_offset(a3[half:], Z, -1)
    return acts, a1, a3, a2, b2


def sum_layers(own, up, down, a1, b3):
    half = a1.shape[0]
    up = to_offset(up, Z, 1)
    down = to_offset(down, Z, -1)
    gate = (up, down)
    a1 = to_offset((a1.astype(F32) + up[:half].astype(F32)).astype(BF16), Z, 1)
    b3 = to_offset((b3.astype(F32) + down[half:].astype(F32)).astype(BF16), Z, -1)
    first = own[:half].astype(F32) + a1.astype(F32) + down[:half].astype(F32)
    second = own[half:].astype(F32) + up[half:].astype(F32) + b3.astype(F32)
    return jnp.concatenate([first, second], axis=0), gate


def per_device(inputs, targets, enc_weight, enc_bias, dec_weight, dec_bias):
    layers, d = dec_bias.shape
    place = jnp.stack([lax.axis_index(axis) for axis in (Z, G, X, Y, C)]).astype(jnp.int32)
    tok_dev = inputs.shape[1]
    total_tokens = tok_dev * lax.axis_size(FEAT) * lax.axis_size(G)
    feats = dec_weight.shape[1]
    decoder = dec_weight.transpose(0, 2, 1).reshape(-1, feats)

    def forward(chunk):
        joined, acts, mask, _ = encode(place, chunk, enc_weight[0], enc_bias)
        sources = gather_layers(acts)
        return (joined, mask, sources), acts

    near, far = gather_rows(inputs[0], forward)
    other_acts = [from_offset(chunk[2][0], G, 1) for chunk in (near, far)]
    far_acts, *far_rows, token = decode(after(place, *other_acts, *near[2][3:]), far[2], decoder, d)
    acts = []

    def near_after():
        near_acts, *near_rows, _ = decode(place, near[2], decoder, d, (token,))
        acts.extend([near_acts, far_acts])
        return near_rows

    parts = sum_rows(near_after, far_rows)
    scaled = scaled_errors(place, parts, targets, dec_bias, total_tokens)
    other_acts = lax.all_gather(jnp.concatenate(other_acts, axis=0), Z, axis=0)

    def backward(chunk):
        *parts, _ = feature_grads(place, chunk, decoder, d)
        dacts, gate = sum_layers(*parts)
        return (chunk, dacts, gate, parts[0]), parts[0]

    other_errors = from_offset(scaled, G, 1)
    graded = gather_rows(scaled, backward, (other_errors,))
    other_errors = lax.all_gather(after(other_errors, *graded[1][0][2:], other_acts), FEAT, axis=0)
    dpre = [jnp.where(c[1] > 0, g[1], jnp.zeros_like(g[1])) for c, g in zip((near, far), graded)]
    enc_bias_grad = sum(jnp.sum(x, axis=0) for x in dpre)
    dpre = [x.astype(BF16) for x in dpre]
    rows = [near[0], far[0]]
    sent = encoder_grad(place, rows, dpre, False, BF16)
    kept = encoder_grad(after(place, sent), rows, dpre, True, F32)
    other_bias_grad = from_offset(enc_bias_grad, G, 1)
    own_errors = [*graded[0][0], *graded[1][0]]
    dec_grad, error_sums, _ = own_pairs_grad(after(place, sent), acts, own_errors, other_acts, other_errors, d)
    enc_grad = (kept + after(from_offset(sent, G, 1), error_sums).astype(F32)).astype(BF16)
    enc_bias_grad = enc_bias_grad + after(other_bias_grad, error_sums)
    return (
        enc_grad[None],
        enc_bias_grad[None],
        dec_grad.transpose(0, 2, 1),
        error_sums[0].reshape(layers, d),
    )


def solution(mesh):
    finer = Mesh(
        mesh.devices.reshape(mesh.shape["grp"], mesh.shape["layer"], 2, 4, 2),
        (G, Z, X, Y, C),
    )
    return jax.shard_map(
        per_device,
        mesh=finer,
        in_specs=(
            P(Z, GRP_FEAT, None),
            P(GRP_FEAT, None, Z),
            P(Z, None, FEAT),
            P(Z, FEAT),
            P(None, FEAT, Z),
            P(None, Z),
        ),
        out_specs=(P(Z, G, FEAT), P(Z, FEAT), P(G, FEAT, Z), P(None, Z)),
        check_vma=False,
    )
```

```python
import jax
import jax.numpy as jnp
from jax import lax
from jax.experimental import pallas as pl
from jax.experimental.pallas import tpu as pltpu
from jax.sharding import Mesh
from jax.sharding import PartitionSpec as P

X, Y, C, Z, G = ("feat_0", "feat_1", "feat_2", "layer", "grp")
FEAT = (X, Y, C)
GRP_FEAT = (G, X, Y, C)
BF16, F32 = (jnp.bfloat16, jnp.float32)
VMEM = pl.BlockSpec(memory_space=pltpu.VMEM)
ANY = pl.BlockSpec(memory_space=pl.ANY)
SMEM = pl.BlockSpec(memory_space=pltpu.SMEM)


def from_offset(x, axis, offset):
    size = lax.axis_size(axis)
    return lax.ppermute(x, axis, [((i + offset) % size, i) for i in range(size)])


def to_offset(x, axis, offset):
    return from_offset(x, axis, -offset)


def after(x, *earlier):
    return lax.optimization_barrier((x, *earlier))[0]


def size_of(shape, dtype):
    count = jnp.dtype(dtype).itemsize
    for n in shape:
        count *= n
    return count


def call(body, outs, place, args, scratch=(), flops=0, wait=(), copies=0):
    outs = [*outs, ((8, 128), F32)]
    moved = sum(size_of(a.shape, a.dtype) for a in args) + sum(size_of(*o) for o in outs)
    held = moved + sum(size_of(*s) for s in scratch)
    first, last = 1 + len(args), 1 + len(args) + len(wait)
    sems = [pltpu.SemaphoreType.DMA((copies,))] if copies else []

    def run(*refs):
        body(*refs[:first], *refs[last:])

    return pl.pallas_call(
        run,
        out_shape=[jax.ShapeDtypeStruct(s, d) for s, d in outs],
        in_specs=[SMEM] + [ANY if copies else VMEM] * (len(args) + len(wait)),
        out_specs=[VMEM] * len(outs),
        scratch_shapes=[pltpu.VMEM(s, d) for s, d in scratch] + sems,
        cost_estimate=pl.CostEstimate(flops=flops, bytes_accessed=moved, transcendentals=0),
        compiler_params=pltpu.CompilerParams(vmem_limit_bytes=60 << 20 if copies else held + (4 << 20)),
    )(place, *args, *wait)


def lay_rows(parts, target):
    at = 0
    for part in parts:
        target[at : at + part.shape[0], :] = part[...]
        at += part.shape[0]


def encode(place, blocks, weight, bias):
    rows = sum(b.shape[0] for b in blocks)
    width, feats = weight.shape
    n = len(blocks)

    def body(_, *refs):
        parts, (w, b, joined, acts, mask, token) = refs[:n], refs[n:]
        token[...] = jnp.zeros_like(token)
        lay_rows(parts, joined)
        pre = jnp.dot(joined[...], w[...], preferred_element_type=F32) + b[...]
        acts[...] = jnp.maximum(pre, 0.0).astype(BF16)
        mask[...] = jnp.where(pre > 0, 1.0, 0.0).astype(BF16)

    return call(
        body,
        [((rows, width), BF16), ((rows, feats), BF16), ((rows, feats), BF16)],
        place,
        [*blocks, weight, bias],
        flops=2 * rows * width * feats,
    )


def fresh(x, edge):
    lane = lax.broadcasted_iota(jnp.int32, x.shape, 1)
    return jnp.where(lane >= edge, x, jnp.zeros_like(x))


def nt(a, b):
    return lax.dot_general(a, b, (((1,), (1,)), ((), ())), preferred_element_type=F32)


def nn(a, b):
    return jnp.dot(a, b, preferred_element_type=F32)


def decode(place, sources, weight, block, wait=()):
    rows, feats = sources[0].shape
    half = rows // 2
    d = block
    wide = 4 * d
    e = d % 128

    def body(at_ref, *refs):
        a0, a1, a3, a2, b2, w, acts, keep, send, token = refs
        token[...] = jnp.zeros_like(token)
        for step, part in ((0, a0), (1, a1), (3, a3)):
            acts[lax.rem(at_ref[0] + step, 4)] = part[...]
        layer = lax.rem(at_ref[0] + 2, 4)
        acts[layer, :half, :] = a2[...]
        acts[layer, half:, :] = b2[...]
        for at, out in ((half, send), (0, keep)):
            a = [acts[s, at : at + half, :] for s in range(4)]
            out[:, : d - e] = nt(a[0], w[: d - e, :]).astype(BF16)
            part = nt(a[0], w[d - e : 2 * d, :]) + fresh(nt(a[1], w[4 * d - e : 5 * d, :]), e)
            out[:, d - e : 2 * d] = part.astype(BF16)
            part = (
                nt(a[0], w[2 * d : 3 * d - e, :])
                + nt(a[1], w[5 * d : 6 * d - e, :])
                + nt(a[2], w[7 * d : 8 * d - e, :])
            )
            out[:, 2 * d : 3 * d - e] = part.astype(BF16)
            part = (
                nt(a[0], w[3 * d - e : 4 * d, :])
                + nt(a[1], w[6 * d - e : 7 * d, :])
                + nt(a[2], w[8 * d - e : 9 * d, :])
                + fresh(nt(a[3], w[9 * d - e :, :]), e)
            )
            out[:, 3 * d - e :] = part.astype(BF16)

    return call(
        body,
        [((4, rows, feats), BF16), ((half, wide), BF16), ((half, wide), BF16)],
        place,
        [*sources, weight],
        flops=20 * rows * feats * d,
        wait=wait,
    )


def feature_grads(place, blocks, weight, block):
    rows = sum(b.shape[0] for b in blocks)
    feats = weight.shape[1]
    d = block
    e = d % 128
    half = rows // 2
    n = len(blocks)

    def body(at_ref, *refs):
        parts, (w, own, up, down, a1, b3, token, held, joined) = refs[:n], refs[n:]
        token[...] = jnp.zeros_like(token)
        lay_rows(parts, joined)

        def slot(layer):
            return lax.rem(layer + 4 - at_ref[0], 4)

        x = joined[...]
        held[slot(0)] = nn(x, w[: 4 * d, :]).astype(BF16)
        part = jnp.concatenate([fresh(x[:, d - e : d - e + 128], e), x[:, d - e + 128 :]], axis=1)
        held[slot(1)] = nn(part, w[4 * d - e : 7 * d, :]).astype(BF16)
        held[slot(2)] = nn(x[:, 2 * d :], w[7 * d : 9 * d, :]).astype(BF16)
        part = jnp.concatenate([fresh(x[:, 3 * d - e : 3 * d - e + 128], e), x[:, 3 * d - e + 128 :]], axis=1)
        held[slot(3)] = nn(part, w[9 * d - e :, :]).astype(BF16)
        own[...] = held[0]
        up[:half, :] = held[2, :half, :]
        up[half:, :] = held[1, half:, :]
        down[:half, :] = held[3, :half, :]
        down[half:, :] = held[2, half:, :]
        a1[...] = held[1, :half, :]
        b3[...] = held[3, half:, :]

    return call(
        body,
        [((rows, feats), BF16)] * 3 + [((half, feats), BF16)] * 2,
        place,
        [*blocks, weight],
        scratch=[((4, rows, feats), BF16), ((rows, 4 * d), BF16)],
        flops=20 * rows * feats * d,
    )


NEAR = ((0, 0), (1, 0), (0, 1), (0, 3))
FAR = ((1, 1), (1, 3), (0, 2), (1, 2))
PAIRS = tuple((s, t) for s in range(4) for t in range(s, 4))


def encoder_grad(place, rows, grads, mine, dtype):
    half, feats = rows[0].shape[1] // 2, grads[0].shape[1]

    def body(at_ref, r0, r1, g0, g1, out, token):
        token[...] = jnp.zeros_like(token)
        part = at_ref[1] if mine else 1 - at_ref[1]
        cut = pl.ds(pl.multiple_of(part * half, 128), half)
        out[...] = (nn(r0[:, cut].T, g0[...]) + nn(r1[:, cut].T, g1[...])).astype(dtype)

    flops = 4 * rows[0].shape[0] * half * feats
    return call(body, [((half, feats), dtype)], place, [*rows, *grads], flops=flops)[0]


def own_pairs_grad(place, acts, errors, other_acts, other_errors, block):
    _, rows, feats = acts[0].shape
    d = block
    wide = 4 * d
    count = 2 * rows
    tokens = other_errors.shape[1]
    own = len(PAIRS) // 2
    pieces, blocks = len(errors), other_errors.shape[0]
    copies = pieces + blocks + 3

    def body(at_ref, a0, a1, *refs):
        parts, refs = refs[:pieces], refs[pieces:]
        a2, others, out, total, token, turned, here, there, acts_here, acts_there, sems = refs
        token[...] = jnp.zeros_like(token)
        first, second, third, at = [], [], [], 0
        for part in parts:
            first.append((part, here.at[pl.ds(at, part.shape[0])]))
            at += part.shape[0]
        at = 0
        for chunk in (NEAR, FAR):
            for core in range(2):
                for dx, dy in chunk:
                    x = lax.rem(at_ref[2] + dx, 2)
                    y = lax.rem(at_ref[3] + dy, 4)
                    c = lax.rem(at_ref[4] + core, 2)
                    second.append((others.at[(x * 4 + y) * 2 + c], there.at[pl.ds(at, tokens)]))
                    at += tokens
        third.append((a0, acts_here.at[:, pl.ds(0, rows)]))
        third.append((a1, acts_here.at[:, pl.ds(rows, rows)]))
        third.append((a2, acts_there))
        moves = [pltpu.make_async_copy(*m, sems.at[k]) for k, m in enumerate(first + second + third)]
        for move in moves:
            move.start()
        sums = jnp.zeros((8, wide), F32)
        cuts = (moves[:pieces], moves[pieces : pieces + blocks])
        for k, (x_ref, awaited) in enumerate(zip((here, there), cuts)):
            for move in awaited:
                move.wait()
            for at in range(0, count, rows):
                x = x_ref[at : at + rows, :]
                sums += nn(jnp.ones((8, rows), BF16), x)
                for t in range(4):
                    low = t * d // 128 * 128
                    start = k * count + at
                    turned[t, :, start : start + rows] = x[:, low : (t + 1) * d].T[t * d - low :]
        total[...] = sums
        for move in moves[pieces + blocks :]:
            move.wait()
        mine = at_ref[1] == 0
        for i in range(own):
            s, t = [jnp.where(mine, m, n) for m, n in zip(PAIRS[i], PAIRS[own + i])]
            part = nn(turned[t, :, :count], acts_here[s]) + nn(turned[t, :, count:], acts_there[s])
            out[i] = part.astype(BF16)

    return call(
        body,
        [((own, d, feats), BF16), ((8, wide), F32)],
        place,
        [*acts, *errors, other_acts, other_errors],
        scratch=[((4, d, 2 * count), BF16)] + [((count, wide), BF16)] * 2 + [((4, count, feats), BF16)] * 2,
        flops=20 * count * feats * d,
        copies=copies,
    )


def gather_rows(block, use, also=()):
    x1 = from_offset(block, X, 1)
    y1 = from_offset(block, Y, 1)
    y3 = from_offset(block, Y, -1)
    near = jnp.concatenate([block, x1, y1, y3], axis=0)
    near_core = from_offset(near, C, 1)
    xy1 = from_offset(y1, X, 1)
    xy3 = from_offset(x1, Y, -1)
    y2 = from_offset(y1, Y, 1)
    xy2 = from_offset(xy1, Y, 1)
    first, made = use([near, near_core])
    y2, xy2 = after((y2, xy2), made, *also)
    far = jnp.concatenate([xy1, xy3, y2], axis=0)
    far_core = from_offset(far, C, 1)
    xy2_core = from_offset(xy2, C, 1)
    return first, use([far, xy2, far_core, xy2_core])[0]


def sum_rows(near_after, far):
    rows = far[0].shape[0] // 4

    def taken(pair, arrived, k):
        cut = slice(k * rows, (k + 1) * rows)
        return pair[cut].astype(F32) + arrived[cut].astype(F32)

    far_in = from_offset(far[1], C, 1)
    q11, q13, q02, q12 = [taken(far[0], far_in, k) for k in range(4)]
    r12 = to_offset(q12.astype(BF16), Y, 1)
    r13 = to_offset(q13.astype(BF16), Y, -1)
    r02 = to_offset(q02.astype(BF16), Y, 1)
    near = near_after()
    near_in = from_offset(near[1], C, 1)
    q00, q10, q01, q03 = [taken(near[0], near_in, k) for k in range(4)]
    r11 = to_offset((q11 + r12.astype(F32)).astype(BF16), X, 1)
    r03 = to_offset(q03.astype(BF16), Y, -1)
    q01 = q01 + r11.astype(F32) + r02.astype(F32)
    q10 = q10 + r13.astype(F32)
    r01 = to_offset(q01.astype(BF16), Y, 1)
    r10 = to_offset(q10.astype(BF16), X, 1)
    return q00, r03, r01, r10


def scaled_errors(place, parts, targets, bias, tokens):
    rows, layers, d = targets.shape

    def body(_, a, b, c, e, targets_ref, bias_ref, out, token):
        token[...] = jnp.zeros_like(token)
        total = a[...] + b[...].astype(F32) + c[...].astype(F32) + e[...].astype(F32)
        wanted = [targets_ref[:, t, :].astype(F32) - bias_ref[t : t + 1, :] for t in range(layers)]
        out[...] = ((total - jnp.concatenate(wanted, axis=1)) / tokens).astype(BF16)

    return call(body, [((rows, layers * d), BF16)], place, [*parts, targets, bias])[0]


def gather_layers(acts):
    half = acts.shape[0] // 2
    a1 = from_offset(acts, Z, 1)
    a3 = from_offset(acts, Z, -1)
    a2 = from_offset(a1[:half], Z, 1)
    b2 = from_offset(a3[half:], Z, -1)
    return acts, a1, a3, a2, b2


def sum_layers(own, up, down, a1, b3):
    half = a1.shape[0]
    up = to_offset(up, Z, 1)
    down = to_offset(down, Z, -1)
    gate = (up, down)
    a1 = to_offset((a1.astype(F32) + up[:half].astype(F32)).astype(BF16), Z, 1)
    b3 = to_offset((b3.astype(F32) + down[half:].astype(F32)).astype(BF16), Z, -1)
    first = own[:half].astype(F32) + a1.astype(F32) + down[:half].astype(F32)
    second = own[half:].astype(F32) + up[half:].astype(F32) + b3.astype(F32)
    return jnp.concatenate([first, second], axis=0), gate


def per_device(inputs, targets, enc_weight, enc_bias, dec_weight, dec_bias):
    layers, d = dec_bias.shape
    place = jnp.stack([lax.axis_index(axis) for axis in (Z, G, X, Y, C)]).astype(jnp.int32)
    tok_dev = inputs.shape[1]
    total_tokens = tok_dev * lax.axis_size(FEAT) * lax.axis_size(G)
    feats = dec_weight.shape[1]
    decoder = dec_weight.transpose(0, 2, 1).reshape(-1, feats)

    def forward(chunk):
        joined, acts, mask, _ = encode(place, chunk, enc_weight[0], enc_bias)
        sources = gather_layers(acts)
        return (joined, mask, sources), acts

    near, far = gather_rows(inputs[0], forward)
    other_acts = [from_offset(chunk[2][0], G, 1) for chunk in (near, far)]
    far_acts, *far_rows, token = decode(after(place, *other_acts, *near[2][3:]), far[2], decoder, d)
    acts = []

    def near_after():
        near_acts, *near_rows, _ = decode(place, near[2], decoder, d, (token,))
        acts.extend([near_acts, far_acts])
        return near_rows

    parts = sum_rows(near_after, far_rows)
    scaled = scaled_errors(place, parts, targets, dec_bias, total_tokens)
    other_acts = lax.all_gather(jnp.concatenate(other_acts, axis=0), Z, axis=0)

    def backward(chunk):
        *parts, _ = feature_grads(place, chunk, decoder, d)
        dacts, gate = sum_layers(*parts)
        return (chunk, dacts, gate, parts[0]), parts[0]

    other_errors = from_offset(scaled, G, 1)
    graded = gather_rows(scaled, backward, (other_errors,))
    other_errors = lax.all_gather(after(other_errors, graded[1][3], other_acts), FEAT, axis=0)
    dpre = [jnp.where(c[1] > 0, g[1], jnp.zeros_like(g[1])) for c, g in zip((near, far), graded)]
    enc_bias_grad = sum(jnp.sum(x, axis=0) for x in dpre)
    dpre = [x.astype(BF16) for x in dpre]
    rows = [near[0], far[0]]
    sent = encoder_grad(place, rows, dpre, False, BF16)
    kept = encoder_grad(after(place, sent), rows, dpre, True, F32)
    other_bias_grad = from_offset(enc_bias_grad, G, 1)
    own_errors = [*graded[0][0], *graded[1][0]]
    dec_grad, error_sums, _ = own_pairs_grad(after(place, sent), acts, own_errors, other_acts, other_errors, d)
    enc_grad = (kept + after(from_offset(sent, G, 1), error_sums).astype(F32)).astype(BF16)
    enc_bias_grad = enc_bias_grad + after(other_bias_grad, error_sums)
    return (
        enc_grad[None],
        enc_bias_grad[None],
        dec_grad.transpose(0, 2, 1),
        error_sums[0].reshape(layers, d),
    )


def solution(mesh):
    finer = Mesh(
        mesh.devices.reshape(mesh.shape["grp"], mesh.shape["layer"], 2, 4, 2),
        (G, Z, X, Y, C),
    )
    return jax.shard_map(
        per_device,
        mesh=finer,
        in_specs=(
            P(Z, GRP_FEAT, None),
            P(GRP_FEAT, None, Z),
            P(Z, None, FEAT),
            P(Z, FEAT),
            P(None, FEAT, Z),
            P(None, Z),
        ),
        out_specs=(P(Z, G, FEAT), P(Z, FEAT), P(G, FEAT, Z), P(None, Z)),
        check_vma=False,
    )
```
